32 devices in a mesh: parts: 2 (over y), dp: 4 (over z), filt: 4 (over x, core).
Axes of the slice: x: 2, y: 2, z: 4, core: 2. Of those that a mesh axis runs over, the one named last changes fastest.
Arguments:
- inputs: bfloat16 [1008, 8, 576], P('filt', ('parts', 'dp')), parts along dimension 1, may hold values from -6 to 6
- filters: bfloat16 [128, 9, 63, 252], P(('parts', 'dp'), None, None, 'filt'), parts along dimension 0, may hold values from -0.0625 to 0.0625
- out_grad: bfloat16 [1008, 8, 576], P('filt', ('parts', 'dp')), parts along dimension 1, may hold values from -6 to 6
- block_owner: int32 [128], P('parts'), parts along dimension 0, may hold values from 0 to 63, each once
Outputs:
- conv_out: bfloat16 [1008, 8, 576], P('filt', ('parts', 'dp')), parts along dimension 1
- in_grad: bfloat16 [1008, 8, 576], P('filt', ('parts', 'dp')), parts along dimension 1
The draws below stay inside these ranges and needn't reach their ends.
There are 2 independent parts, one for each index of `parts`. The reference program is written for one: setup_inputs(seed, part) draws one part's arguments, and reference() takes and returns one part's arrays. A program takes and returns all parts, laid end to end along the dimension named above; each array names one. Nothing has to cross between parts.
Inputs may be any that keep to these rules, and one draw needn't show every extreme that they name: `block_owner`: each slot holds exactly one block; slots are split evenly and in order along dp.
All inputs are finite; a program needn't handle non-finite values.
Results may differ from the reference program's by a relative error of at most 0.001.
Values may be sent and summed in bfloat16 or wider, within the bound.
A program may use at most 64 MiB of HBM per device.

```python
import jax
import jax.numpy as jnp

GW = 1008
HH = 24
WW = 24
CO_SPLIT = 4
CI_SPLIT = 16
IMAGES = 4
PIX = 576
COB = 63
CIB = 63
NBLK = 64
N_FILT = 4


def levels(rng, shape, cuts, low, top_value):
    def one(axis_at, blocks):
        heights = jax.random.uniform(jax.random.fold_in(jax.random.fold_in(rng, 6), axis_at), (blocks,), jnp.float32, low / len(cuts), top_value / len(cuts))
        return jnp.repeat(jnp.exp(heights), shape[axis_at] // blocks).reshape((-1,) + (1,) * (len(shape) - axis_at - 1))

    loudness = one(*cuts[0])
    for cut in cuts[1:]:
        loudness = loudness * one(*cut)
    return loudness


def noise(own_key, dims, width, limit, split=(), kind=jnp.bfloat16):
    factor_of = levels(own_key, dims, split, -0.22, 0.18) if split else 1.0
    array = jax.random.normal(own_key, dims, jnp.float32) * width * factor_of
    return jnp.minimum(jnp.maximum(array, -limit), limit).astype(kind)


def setup_inputs(seed: int = 0, part: int = 0) -> dict:
    seeds = jax.random.split(jax.random.key(seed), 5)
    part_splits = jax.random.split(jax.random.fold_in(seeds[4], part), 5)
    inputs = noise(part_splits[0], (GW, IMAGES, PIX), 1.0, 6.0, ((0, 4), (1, 4)))
    filters = noise(part_splits[1], (NBLK, 9, CIB, N_FILT * COB), (9 * GW) ** -0.5, 0.0625, ((0, 4), (3, 4)))
    out_grad = noise(part_splits[2], (GW, IMAGES, PIX), 1.0, 6.0, ((0, 4), (1, 4)))
    block_owner = jax.random.permutation(part_splits[3], NBLK).astype(jnp.int32)
    return {"inputs": inputs, "filters": filters, "out_grad": out_grad, "block_owner": block_owner}


def assemble(filters, block_owner):
    ordered = jnp.take(filters, block_owner.astype(jnp.int32), axis=0)
    ordered = ordered.reshape(CO_SPLIT, CI_SPLIT, 9, CIB, N_FILT, COB)
    return ordered.transpose(2, 1, 3, 4, 0, 5).reshape(9, GW, GW)


def tap_window(flat, shift_row, shift_col):
    padded = jnp.pad(flat, ((0, 0), (0, 0), (WW + 1, WW + 1)))
    begin = (WW + 1) + (shift_row - 1) * WW + (shift_col - 1)
    piece = padded[:, :, begin:begin + HH * WW]
    column = jnp.arange(HH * WW, dtype=jnp.int32) % WW + (shift_col - 1)
    valid = (column >= 0) & (column < WW)
    piece = jnp.where(valid[None, None, :], piece, jnp.zeros_like(piece))
    return piece.reshape(flat.shape[0], flat.shape[1] * HH * WW)


def reference(inputs, filters, out_grad, block_owner):
    weights = assemble(filters, block_owner)
    forward_sum = jnp.zeros((GW, IMAGES * PIX), jnp.float32)
    backward_sum = jnp.zeros((GW, IMAGES * PIX), jnp.float32)
    for offset in range(9):
        shift_row = offset // 3
        shift_col = offset % 3
        window = tap_window(inputs, shift_row, shift_col)
        forward_sum = forward_sum + jnp.dot(weights[offset].T, window, preferred_element_type=jnp.float32)
        back_window = tap_window(out_grad, 2 - shift_row, 2 - shift_col)
        backward_sum = backward_sum + jnp.dot(weights[offset], back_window, preferred_element_type=jnp.float32)
    conv_out = forward_sum.reshape(GW, IMAGES, PIX).astype(jnp.bfloat16)
    in_grad = backward_sum.reshape(GW, IMAGES, PIX).astype(jnp.bfloat16)
    return (conv_out, in_grad)
```

```python
import functools

import jax
import jax.numpy as jnp
from jax import lax
from jax.experimental import pallas as pl
from jax.experimental.pallas import tpu as pltpu
from jax.sharding import PartitionSpec as P

GW = 1008
HH = 24
WW = 24
CO_SPLIT = 4
CI_SPLIT = 16
CIB = 63
TAPS = 9
SLAB = 64
LANES = 128
MESH = pl.DeviceIdType.MESH
F32 = jnp.float32
BF16 = jnp.bfloat16


def tap_window(flat, shift_row, shift_col):
    padded = jnp.pad(flat, ((0, 0), (0, 0), (WW + 1, WW + 1)))
    begin = WW + 1 + (shift_row - 1) * WW + (shift_col - 1)
    piece = padded[:, :, begin : begin + HH * WW]
    column = jnp.arange(HH * WW, dtype=jnp.int32) % WW + (shift_col - 1)
    valid = (column >= 0) & (column < WW)
    piece = jnp.where(valid[None, None, :], piece, jnp.zeros_like(piece))
    return piece.reshape(flat.shape[0], flat.shape[1] * HH * WW)


def plain_body(inputs, filters, out_grad, block_owner):
    slot_data = lax.all_gather(filters, "dp", axis=0, tiled=True)
    blocks = lax.map(lambda b: lax.dynamic_index_in_dim(slot_data, b, 0, False), block_owner)
    col_block = filters.shape[3]
    w_local = blocks.reshape(CO_SPLIT, CI_SPLIT, TAPS, CIB, col_block)
    w_local = w_local.transpose(2, 1, 3, 0, 4).reshape(TAPS, GW, CO_SPLIT * col_block)
    image_total = inputs.shape[1]
    pixel_span = image_total * HH * WW
    running = jnp.zeros((w_local.shape[2], pixel_span), F32)
    portion = lax.all_gather(inputs, "filt", axis=0, tiled=True)
    for offset in range(TAPS):
        window = tap_window(portion, offset // 3, offset % 3)
        running = running + lax.dot_general(
            w_local[offset], window, (((0,), (0,)), ((), ())), preferred_element_type=F32
        )
    conv_out = running.reshape(running.shape[0], image_total, HH * WW).astype(BF16)
    total_sum = jnp.zeros((inputs.shape[0] * lax.axis_size("filt"), pixel_span), F32)
    for offset in range(TAPS):
        window = tap_window(out_grad, 2 - offset // 3, 2 - offset % 3)
        total_sum = total_sum + jnp.dot(w_local[offset], window, preferred_element_type=F32)
    result = lax.psum_scatter(total_sum, "filt", scatter_dimension=0, tiled=True)
    in_grad = result.reshape(result.shape[0], image_total, HH * WW).astype(BF16)
    return (conv_out, in_grad)


def main_kernel(
    x_ref, g_ref, f_ref, owner_ref, conv_ref, grad_ref,
    fbuf, tmp2, tmp, wbuf, cur, wt, wg, ch, win, mask, acc_c, acc_g, ret, back,
    fsem, wsend, wrecv, csend, crecv, xsend, xrecv, rsend, rrecv,
):
    me = lax.axis_index("dp")
    f = lax.axis_index("filt")
    taps, rows_in, slots, cols_in = f_ref.shape
    pixels, channels = x_ref.shape
    rows = ret.shape[2]
    pitch = pixels + 2 * WW
    both = pitch + pixels
    F = wt.shape[1] // rows
    half_slab = SLAB // 2
    fx, fc = f // 2, f % 2

    def rel(j):
        j1, j2 = j % 2, j // 2
        return 2 * (fx + j2 - 2 * fx * j2) + (fc + j1 - 2 * fc * j1)

    mate = me + 1 - 2 * (me % 2)
    across = 3 - me
    far = across + 1 - 2 * (across % 2)
    im = ((me + 1) // 2) % 2
    worker = im == 1

    def load_tap(t):
        return pltpu.make_async_copy(f_ref.at[t], fbuf.at[t], fsem.at[t])

    for t in range(taps):
        load_tap(t).start()

    barrier = pltpu.get_barrier_semaphore()
    for j in range(1, F):
        pl.semaphore_signal(barrier, inc=1, device_id={"filt": rel(j)}, device_id_type=MESH)
    pl.semaphore_signal(barrier, inc=1, device_id={"dp": mate}, device_id_type=MESH)

    @pl.when(worker)
    def _():
        pl.semaphore_signal(barrier, inc=1, device_id={"dp": across}, device_id_type=MESH)

    def region(t, o):
        return wbuf.at[t, pl.ds(o * slots, slots)]

    def fcopy(t, o, kind, to):
        return pltpu.make_async_remote_copy(
            src_ref=region(t, o), dst_ref=region(t, o), send_sem=wsend.at[kind, t],
            recv_sem=wrecv.at[kind, t], device_id={"dp": to}, device_id_type=MESH,
        )

    def ccopy(img, q, j, k):
        if k == 3:
            to, device = j, {"dp": mate}
        else:
            to, device = j ^ k, {"filt": rel(k)}
        return pltpu.make_async_remote_copy(
            src_ref=ch.at[img, q, j], dst_ref=ch.at[img, q, to], send_sem=csend.at[k - 1, img, q, j],
            recv_sem=crecv.at[img, q, to], device_id=device, device_id_type=MESH,
        )

    def carrived(img, q, j):
        pltpu.make_async_remote_copy(
            src_ref=ch.at[img, q, j], dst_ref=ch.at[img, q, j], send_sem=csend.at[0, img, q, j],
            recv_sem=crecv.at[img, q, j], device_id={"filt": rel(1)}, device_id_type=MESH,
        ).wait_recv()

    def xcopy(t, j):
        return pltpu.make_async_remote_copy(
            src_ref=wt.at[t, pl.ds(j * rows, rows)], dst_ref=wg.at[t, :, pl.ds(j * rows, rows)],
            send_sem=xsend.at[t, j], recv_sem=xrecv.at[t, j], device_id={"filt": rel(j)}, device_id_type=MESH,
        )

    def rcopy(q):
        return pltpu.make_async_remote_copy(
            src_ref=ret.at[q], dst_ref=back.at[q], send_sem=rsend.at[q],
            recv_sem=rrecv.at[q], device_id={"dp": mate}, device_id_type=MESH,
        )

    tmp2[...] = jnp.zeros_like(tmp2)

    def pack(t):
        load_tap(t).wait()
        tmp2[: rows_in * slots, :cols_in] = fbuf[t].astype(F32).reshape(rows_in * slots, cols_in)
        for s in range(slots):
            lo = tmp2[pl.ds(s, half_slab, stride=slots), :]
            hi = tmp2[pl.ds(half_slab * slots + s, half_slab, stride=slots), :]
            wbuf[t, me * slots + s] = (lo + pltpu.roll(hi, SLAB, 1)).astype(BF16)

    def pack_rest(lo):
        def one(t, carry):
            pack(t)
            return carry

        lax.fori_loop(lo, taps, one, 0)

    tmp[...] = jnp.zeros_like(tmp)
    chan = lax.broadcasted_iota(jnp.int32, (pixels, rows), 1)

    def spread(src, q):
        tmp[:, :channels] = src[...].astype(F32)
        raw = tmp[...]
        v = jnp.zeros_like(raw)
        for k in range(channels // CIB):
            moved = raw if k == 0 else pltpu.roll(raw, k, 1)
            v = jnp.where((chan >= k * SLAB) & (chan < k * SLAB + CIB), moved, v)
        ch[im, q, 0] = v.astype(BF16)

    pack(0)
    pl.semaphore_wait(barrier, F + im)

    @pl.when(im == 0)
    def _():
        fcopy(0, me, 0, mate).start()
        spread(x_ref, 0)
        ccopy(0, 0, 0, 2).start()
        pack(1)
        fcopy(1, me, 0, mate).start()
        ccopy(0, 0, 0, 3).start()
        spread(g_ref, 1)
        ccopy(0, 1, 0, 2).start()
        pack_rest(2)
        flight = [fcopy(0, me, 0, mate), fcopy(1, me, 0, mate), ccopy(0, 0, 0, 3)]

        def go(copy, ahead=2):
            flight[len(flight) - ahead].wait_send()
            copy.start()
            flight.append(copy)

        flight[0].wait_send()
        go(fcopy(2, me, 0, mate))
        carrived(1, 1, 0)
        ccopy(1, 1, 0, 2).start()
        go(fcopy(3, me, 0, mate))
        carrived(0, 0, 2)
        go(ccopy(0, 0, 2, 3))
        go(fcopy(4, me, 0, mate))
        go(fcopy(5, me, 0, mate))
        carrived(1, 1, 2)
        go(ccopy(1, 1, 2, 3))
        go(fcopy(6, me, 0, mate))
        go(fcopy(7, me, 0, mate))
        go(ccopy(0, 1, 0, 3))
        go(fcopy(8, me, 0, mate))
        carrived(0, 1, 2)
        go(ccopy(0, 1, 2, 3))
        for copy in flight[-2:]:
            copy.wait_send()
        for copy in (ccopy(0, 0, 0, 2), ccopy(0, 1, 0, 2), ccopy(1, 1, 0, 2)):
            copy.wait_send()
        rcopy(0).wait_recv()
        conv_ref[...] = back[0]
        rcopy(1).wait_recv()
        grad_ref[...] = back[1]

    @pl.when(worker)
    def _():
        lane = lax.broadcasted_iota(jnp.int32, (half_slab, LANES), 1)

        def assemble(t):
            cur[...] = wbuf[t]

            def one(c, carry):
                block = rel(c // (CI_SPLIT // F)) * (CI_SPLIT // F) + c % (CI_SPLIT // F)
                for p in range(CO_SPLIT // 2):
                    vl = cur[owner_ref[2 * p * CI_SPLIT + block]].astype(F32)
                    vr = cur[owner_ref[(2 * p + 1) * CI_SPLIT + block]].astype(F32)
                    top = jnp.where(lane < SLAB, vl, pltpu.roll(vr, SLAB, 1))
                    low = jnp.where(lane < SLAB, pltpu.roll(vl, SLAB, 1), vr)
                    pair = jnp.concatenate([top, low], axis=0).astype(BF16)
                    wt[t, pl.ds(pl.multiple_of(c * SLAB, SLAB), SLAB), p * LANES : (p + 1) * LANES] = pair
                return carry

            lax.fori_loop(0, CI_SPLIT, one, 0, unroll=4)
            wg[t, :, :rows] = wt[t, :rows]

        def build(q, img, lo, hi):
            edge = jnp.zeros((WW, LANES), F32)

            def one(k, carry):
                j = k // (rows // LANES)
                part = pl.ds(pl.multiple_of((k % (rows // LANES)) * LANES, LANES), LANES)
                dst = pl.ds(pl.multiple_of(k * LANES, LANES), LANES)
                raw = ch[img, q, j, :, part].astype(F32)
                for d in range(3):
                    if d == 1:
                        v = raw
                    else:
                        moved = pltpu.roll(raw, 1 if d == 0 else pixels - 1, 0)
                        v = jnp.where(mask[d // 2] > 0, moved, 0.0)
                    at = img * pitch
                    win[q, 1, d, pl.ds(pl.multiple_of(at, 16), pixels), dst] = v.astype(BF16)
                    tall = jnp.concatenate([edge, v, edge], axis=0).astype(BF16)
                    win[q, 0, d, pl.ds(pl.multiple_of(at, 16), pitch), dst] = tall
                return carry

            lax.fori_loop(lo, hi, one, 0)

        def conv(t, carry):
            r, c = t // 3, t % 3
            start = pl.multiple_of(r // 2 * 2 * WW, 16)
            acc_c[...] += jnp.dot(win[0, r % 2, c, pl.ds(start, both), :], wt[t], preferred_element_type=F32)
            return carry

        def grads(img, lo, n):
            at = pl.ds(pl.multiple_of(lo * rows, rows), n * rows)

            def one(t, carry):
                r, c = 2 - t // 3, 2 - t % 3
                start = pl.multiple_of(img * pitch + r // 2 * 2 * WW, 16)
                acc_g[img] += lax.dot_general(
                    win[1, r % 2, c, pl.ds(start, pixels), at], wg[t, :, at],
                    (((1,), (1,)), ((), ())), preferred_element_type=F32,
                )
                return carry

            return one

        def wex(t, carry):
            for j in range(1, F):
                xcopy(t, j).wait_recv()
            return carry

        fcopy(0, me, 1, across).start()
        spread(x_ref, 0)
        ccopy(1, 0, 0, 2).start()
        ccopy(1, 0, 0, 1).start()
        pack(1)
        fcopy(1, me, 1, across).start()
        spread(g_ref, 1)
        ccopy(1, 1, 0, 3).start()
        ccopy(1, 1, 0, 1).start()
        pack_rest(2)

        def forward(t):
            fcopy(t, mate, 0, mate).wait_recv()
            fcopy(t, mate, 2, across).start()

        forward(0)
        fcopy(2, me, 1, across).start()
        acc_c[...] = jnp.zeros_like(acc_c)
        acc_g[...] = jnp.zeros_like(acc_g)
        for q in range(2):
            for d in range(3):
                win[q, 1, d, pixels:pitch] = jnp.zeros((pitch - pixels, F * rows), BF16)
        col = lax.broadcasted_iota(jnp.int32, (pixels, LANES), 0) % WW
        mask[0] = jnp.where(col >= 1, 1.0, 0.0)
        mask[1] = jnp.where(col < WW - 1, 1.0, 0.0)
        carrived(1, 0, 2)
        ccopy(1, 0, 2, 1).start()
        forward(1)
        fcopy(3, me, 1, across).start()
        carrived(1, 0, 1)
        carrived(1, 1, 1)
        carrived(1, 0, 3)

        def step(t, carry):
            @pl.when((t >= 1) & (t + 1 < taps))
            def _():
                forward(t + 1)

            @pl.when((t >= 1) & (t + 3 < taps))
            def _():
                fcopy(t + 3, me, 1, across).start()

            @pl.when(t == 2)
            def _():
                carrived(0, 0, 0)
                ccopy(0, 0, 0, 1).start()

            @pl.when(t == 3)
            def _():
                carrived(0, 0, 2)
                ccopy(0, 0, 2, 1).start()

            @pl.when(t == 5)
            def _():
                carrived(1, 1, 2)
                ccopy(1, 1, 2, 1).start()

            @pl.when(t == 7)
            def _():
                carrived(0, 1, 0)
                ccopy(0, 1, 0, 1).start()

            fcopy(t, across, 1, across).wait_recv()
            fcopy(t, far, 2, across).wait_recv()
            assemble(t)
            for j in (2, 3, 1):
                xcopy(t, j).start()

            @pl.when(t == 3)
            def _():
                carrived(0, 0, 1)
                carrived(0, 0, 3)

            @pl.when(t == 5)
            def _():
                carrived(1, 1, 3)

            @pl.when(t == 7)
            def _():
                carrived(0, 1, 1)

            parts = rows // LANES * F
            early = (t == 0) | (t == 3) | (t == 5)
            count = jnp.where(early, parts, jnp.where(t == 7, parts // 2, 0))
            build(t // 5, jnp.where((t == 0) | (t == 5), 1, 0), 0, count)
            lax.fori_loop(jnp.where(t == 3, 0, t), jnp.where(t >= 3, t + 1, 0), conv, 0)

            lo = jnp.where(t == 5, 0, t - 2)
            hi = jnp.where(t >= 5, t - 1, lo)
            lax.fori_loop(lo, hi, wex, 0)
            lax.fori_loop(lo, hi, grads(1, 0, F), 0)
            lo0 = jnp.where(t == 7, 0, t - 2)
            hi0 = jnp.where(t >= 7, t - 1, lo0)
            lax.fori_loop(lo0, hi0, grads(0, 0, F // 2), 0)
            return carry

        lax.fori_loop(0, taps, step, 0)
        ret[0] = acc_c[:pixels].astype(BF16)
        rcopy(0).start()
        carrived(0, 1, 2)
        ccopy(0, 1, 2, 1).start()
        conv_ref[...] = acc_c[pitch:].astype(BF16)
        carrived(0, 1, 3)
        parts = rows // LANES * F
        build(1, 0, parts // 2, parts)
        lax.fori_loop(0, taps - 2, grads(0, F // 2, F // 2), 0)
        wex(taps - 2, 0)
        wex(taps - 1, 0)
        lax.fori_loop(taps - 2, taps, grads(0, 0, F), 0)
        ret[1] = acc_g[0].astype(BF16)
        rcopy(1).start()
        lax.fori_loop(taps - 2, taps, grads(1, 0, F), 0)
        grad_ref[...] = acc_g[1].astype(BF16)

        def drain(t, carry):
            fcopy(t, me, 1, across).wait_send()
            fcopy(t, mate, 2, across).wait_send()
            for j in range(1, F):
                xcopy(t, j).wait_send()
            return carry

        lax.fori_loop(0, taps, drain, 0)
        for args in (
            (1, 0, 0, 2), (1, 0, 0, 1), (1, 1, 0, 3), (1, 1, 0, 1), (1, 0, 2, 1), (0, 0, 0, 1),
            (0, 0, 2, 1), (1, 1, 2, 1), (0, 1, 0, 1), (0, 1, 2, 1),
        ):
            ccopy(*args).wait_send()
        rcopy(0).wait_send()
        rcopy(1).wait_send()


def close_kernel(conv_ref, grad_ref, conv_out, grad_out):
    pixels, rows = conv_ref.shape
    channels = conv_out.shape[1]
    lanes = lax.broadcasted_iota(jnp.int32, (pixels, rows), 1)
    for src, dst in ((conv_ref, conv_out), (grad_ref, grad_out)):
        v = src[...].astype(F32)
        out = v
        for k in range(1, channels // CIB):
            out = jnp.where(lanes >= k * CIB, pltpu.roll(v, rows - k, 1), out)
        dst[...] = out.astype(BF16)[:, :channels]


def fast_body(D, F, inputs, filters, out_grad, block_owner):
    slots, taps = filters.shape[0], filters.shape[1]
    channels, images, pixels = inputs.shape
    rows = channels // CIB * SLAB
    pitch = pixels + 2 * WW
    x, g = inputs[:, 0].T, out_grad[:, 0].T
    fl = filters.transpose(1, 2, 0, 3)
    vm = pl.BlockSpec(memory_space=pltpu.VMEM)
    sm = pl.BlockSpec(memory_space=pltpu.SMEM)
    dma = pltpu.SemaphoreType.DMA
    padded = pl.pallas_call(
        main_kernel,
        out_shape=[jax.ShapeDtypeStruct((pixels, rows), BF16)] * 2,
        in_specs=[vm, vm, pl.BlockSpec(memory_space=pl.ANY), sm],
        out_specs=[vm, vm],
        scratch_shapes=[
            pltpu.VMEM(fl.shape, BF16),
            pltpu.VMEM((SLAB * slots, LANES), F32),
            pltpu.VMEM((pixels, rows), F32),
            pltpu.VMEM((taps, D * slots, SLAB // 2, LANES), BF16),
            pltpu.VMEM((D * slots, SLAB // 2, LANES), BF16),
            pltpu.VMEM((taps, F * rows, rows), BF16),
            pltpu.VMEM((taps, rows, F * rows), BF16),
            pltpu.VMEM((2, 2, F, pixels, rows), BF16),
            pltpu.VMEM((2, 2, 3, 2 * pitch, F * rows), BF16),
            pltpu.VMEM((2, pixels, LANES), F32),
            pltpu.VMEM((pitch + pixels, rows), F32),
            pltpu.VMEM((2, pixels, rows), F32),
            pltpu.VMEM((2, pixels, rows), BF16),
            pltpu.VMEM((2, pixels, rows), BF16),
            dma((taps,)), dma((3, taps)), dma((3, taps)), dma((3, 2, 2, F)), dma((2, 2, F)),
            dma((taps, F)), dma((taps, F)), dma((2,)), dma((2,)),
        ],
        compiler_params=pltpu.CompilerParams(
            collective_id=0, has_side_effects=True, vmem_limit_bytes=62 * 1024 * 1024
        ),
    )(x, g, fl, block_owner)
    conv, grad = pl.pallas_call(
        close_kernel,
        out_shape=[jax.ShapeDtypeStruct((pixels, channels), BF16)] * 2,
        in_specs=[vm, vm],
        out_specs=[vm, vm],
    )(*padded)
    return conv.T[:, None], grad.T[:, None]


def solution(mesh):
    D, F = mesh.shape["dp"], mesh.shape["filt"]
    placed = (
        P("filt", ("parts", "dp"), None),
        P(("parts", "dp"), None, None, "filt"),
        P("filt", ("parts", "dp"), None),
        P("parts"),
    )

    def body(inputs, filters, out_grad, block_owner):
        if D == 4 and F == 4 and filters.shape[0] % 16 == 0 and inputs.shape[1] == 1:
            return fast_body(D, F, inputs, filters, out_grad, block_owner)
        return plain_body(inputs, filters, out_grad, block_owner)

    return jax.shard_map(
        body,
        mesh=mesh,
        in_specs=placed,
        out_specs=(P("filt", ("parts", "dp"), None), P("filt", ("parts", "dp"), None)),
        check_vma=False,
    )
```

```python
import functools

import jax
import jax.numpy as jnp
from jax import lax
from jax.experimental import pallas as pl
from jax.experimental.pallas import tpu as pltpu
from jax.sharding import PartitionSpec as P

GW = 1008
HH = 24
WW = 24
CO_SPLIT = 4
CI_SPLIT = 16
CIB = 63
TAPS = 9
SLAB = 64
LANES = 128
MESH = pl.DeviceIdType.MESH
F32 = jnp.float32
BF16 = jnp.bfloat16


def tap_window(flat, shift_row, shift_col):
    padded = jnp.pad(flat, ((0, 0), (0, 0), (WW + 1, WW + 1)))
    begin = WW + 1 + (shift_row - 1) * WW + (shift_col - 1)
    piece = padded[:, :, begin : begin + HH * WW]
    column = jnp.arange(HH * WW, dtype=jnp.int32) % WW + (shift_col - 1)
    valid = (column >= 0) & (column < WW)
    piece = jnp.where(valid[None, None, :], piece, jnp.zeros_like(piece))
    return piece.reshape(flat.shape[0], flat.shape[1] * HH * WW)


def plain_body(inputs, filters, out_grad, block_owner):
    slot_data = lax.all_gather(filters, "dp", axis=0, tiled=True)
    blocks = lax.map(lambda b: lax.dynamic_index_in_dim(slot_data, b, 0, False), block_owner)
    col_block = filters.shape[3]
    w_local = blocks.reshape(CO_SPLIT, CI_SPLIT, TAPS, CIB, col_block)
    w_local = w_local.transpose(2, 1, 3, 0, 4).reshape(TAPS, GW, CO_SPLIT * col_block)
    image_total = inputs.shape[1]
    pixel_span = image_total * HH * WW
    running = jnp.zeros((w_local.shape[2], pixel_span), F32)
    portion = lax.all_gather(inputs, "filt", axis=0, tiled=True)
    for offset in range(TAPS):
        window = tap_window(portion, offset // 3, offset % 3)
        running = running + lax.dot_general(
            w_local[offset], window, (((0,), (0,)), ((), ())), preferred_element_type=F32
        )
    conv_out = running.reshape(running.shape[0], image_total, HH * WW).astype(BF16)
    total_sum = jnp.zeros((inputs.shape[0] * lax.axis_size("filt"), pixel_span), F32)
    for offset in range(TAPS):
        window = tap_window(out_grad, 2 - offset // 3, 2 - offset % 3)
        total_sum = total_sum + jnp.dot(w_local[offset], window, preferred_element_type=F32)
    result = lax.psum_scatter(total_sum, "filt", scatter_dimension=0, tiled=True)
    in_grad = result.reshape(result.shape[0], image_total, HH * WW).astype(BF16)
    return (conv_out, in_grad)


def main_kernel(
    x_ref, g_ref, f_ref, owner_ref, conv_ref, grad_ref,
    fbuf, xin, tmp2, tmp, wbuf, cur, wt, wg, ch, win, mask, perm, acc_c, acc_g, ret, back, outb,
    fsem, isem, osem, wsend, wrecv, csend, crecv, xsend, xrecv, rsend, rrecv,
):
    me = lax.axis_index("dp")
    f = lax.axis_index("filt")
    taps, rows_in, slots, cols_in = f_ref.shape
    pixels, channels = x_ref.shape
    rows = ret.shape[2]
    pitch = pixels + 2 * WW
    both = pitch + pixels
    F = wt.shape[1] // rows
    half_slab = SLAB // 2
    fx, fc = f // 2, f % 2

    def rel(j):
        j1, j2 = j % 2, j // 2
        return 2 * (fx + j2 - 2 * fx * j2) + (fc + j1 - 2 * fc * j1)

    mate = me + 1 - 2 * (me % 2)
    across = 3 - me
    far = across + 1 - 2 * (across % 2)
    im = ((me + 1) // 2) % 2
    worker = im == 1

    def load_tap(t):
        return pltpu.make_async_copy(f_ref.at[t], fbuf.at[t], fsem.at[t])

    def load_in(q):
        return pltpu.make_async_copy((x_ref, g_ref)[q], xin.at[q], isem.at[q])

    def store_out(q):
        return pltpu.make_async_copy(outb.at[q], (conv_ref, grad_ref)[q], osem.at[q])

    load_tap(0).start()
    barrier = pltpu.get_barrier_semaphore()
    for j in range(1, F):
        pl.semaphore_signal(barrier, inc=1, device_id={"filt": rel(j)}, device_id_type=MESH)
    pl.semaphore_signal(barrier, inc=1, device_id={"dp": mate}, device_id_type=MESH)

    @pl.when(worker)
    def _():
        pl.semaphore_signal(barrier, inc=1, device_id={"dp": across}, device_id_type=MESH)

    for t in range(1, taps):
        load_tap(t).start()
    for q in range(2):
        load_in(q).start()

    def fcopy(t, o, kind, to, h):
        part = wbuf.at[t, pl.ds(o * slots + h * (slots // 2), slots // 2)]
        return pltpu.make_async_remote_copy(
            src_ref=part, dst_ref=part, send_sem=wsend.at[kind, t, h],
            recv_sem=wrecv.at[kind, t, h], device_id={"dp": to}, device_id_type=MESH,
        )

    def ccopy(img, q, j, k, h):
        if k == 3:
            to, device = j, {"dp": mate}
        else:
            to, device = j ^ k, {"filt": rel(k)}
        part = pl.ds(h * (pixels // 2), pixels // 2)
        return pltpu.make_async_remote_copy(
            src_ref=ch.at[img, q, j, part], dst_ref=ch.at[img, q, to, part], send_sem=csend.at[k - 1, img, q, j, h],
            recv_sem=crecv.at[img, q, to, h], device_id=device, device_id_type=MESH,
        )

    def csend_all(img, q, j, k):
        for h in range(2):
            ccopy(img, q, j, k, h).start()

    def carrived(img, q, j):
        for h in range(2):
            part = ch.at[img, q, j, pl.ds(h * (pixels // 2), pixels // 2)]
            pltpu.make_async_remote_copy(
                src_ref=part, dst_ref=part, send_sem=csend.at[0, img, q, j, h],
                recv_sem=crecv.at[img, q, j, h], device_id={"filt": rel(1)}, device_id_type=MESH,
            ).wait_recv()

    def xcopy(t, j, h):
        return pltpu.make_async_remote_copy(
            src_ref=wt.at[t, pl.ds(j * rows + h * LANES, LANES)],
            dst_ref=wg.at[t, pl.ds(h * LANES, LANES), pl.ds(j * rows, rows)],
            send_sem=xsend.at[t, j, h], recv_sem=xrecv.at[t, j, h], device_id={"filt": rel(j)}, device_id_type=MESH,
        )

    def rcopy(q, h):
        part = pl.ds(h * LANES, LANES)
        return pltpu.make_async_remote_copy(
            src_ref=ret.at[q, :, part], dst_ref=back.at[q, :, part], send_sem=rsend.at[q, h],
            recv_sem=rrecv.at[q, h], device_id={"dp": mate}, device_id_type=MESH,
        )

    tmp2[...] = jnp.zeros_like(tmp2)

    def pack(t):
        load_tap(t).wait()
        tmp2[: rows_in * slots, :cols_in] = fbuf[t].astype(F32).reshape(rows_in * slots, cols_in)
        for s in range(slots):
            lo = tmp2[pl.ds(s, half_slab, stride=slots), :]
            hi = tmp2[pl.ds(half_slab * slots + s, half_slab, stride=slots), :]
            wbuf[t, me * slots + s] = (lo + pltpu.roll(hi, SLAB, 1)).astype(BF16)

    def pack_rest(lo):
        def one(t, carry):
            pack(t)
            return carry

        lax.fori_loop(lo, taps, one, 0)

    tmp[...] = jnp.zeros_like(tmp)
    chan = lax.broadcasted_iota(jnp.int32, (pixels, rows), 1)

    def spread(q):
        load_in(q).wait()
        tmp[:, :channels] = xin[q].astype(F32)
        raw = tmp[...]
        v = jnp.zeros_like(raw)
        for k in range(channels // CIB):
            moved = raw if k == 0 else pltpu.roll(raw, k, 1)
            v = jnp.where((chan >= k * SLAB) & (chan < k * SLAB + CIB), moved, v)
        ch[im, q, 0] = v.astype(BF16)

    def close(v, q):
        outb[q] = jnp.dot(v, perm[...], preferred_element_type=F32).astype(BF16)[:, :channels]
        store_out(q).start()

    def make_perm():
        src = lax.broadcasted_iota(jnp.int32, (rows, rows), 0)
        dst = lax.broadcasted_iota(jnp.int32, (rows, rows), 1)
        hit = jnp.zeros((rows, rows), F32)
        for k in range(channels // CIB):
            hit = jnp.where((src - dst == k) & (dst >= k * CIB) & (dst < (k + 1) * CIB), 1.0, hit)
        perm[...] = hit.astype(BF16)

    pack(0)
    pl.semaphore_wait(barrier, F + im)

    @pl.when(im == 0)
    def _():
        flight = []

        def go(*copies):
            for copy in copies:
                if len(flight) >= 3:
                    flight[len(flight) - 3].wait_send()
                copy.start()
                flight.append(copy)

        def tap(t):
            go(fcopy(t, me, 0, mate, 0), fcopy(t, me, 0, mate, 1))

        def chunk(img, q, j, *halves):
            go(*[ccopy(img, q, j, 3, h) for h in halves])

        tap(0)
        spread(0)
        csend_all(0, 0, 0, 2)
        pack(1)
        tap(1)
        spread(1)
        csend_all(0, 1, 0, 2)
        pack_rest(2)
        tap(2)
        chunk(0, 0, 0, 0, 1)
        carrived(1, 1, 0)
        csend_all(1, 1, 0, 2)
        tap(3)
        carrived(0, 0, 2)
        chunk(0, 0, 2, 0)
        tap(4)
        chunk(0, 0, 2, 1)
        tap(5)
        chunk(0, 1, 0, 0)
        tap(6)
        chunk(0, 1, 0, 1)
        tap(7)
        tap(8)
        carrived(0, 1, 2)
        chunk(0, 1, 2, 0, 1)
        carrived(1, 1, 2)
        chunk(1, 1, 2, 0, 1)
        make_perm()
        for copy in flight[-3:]:
            copy.wait_send()
        for h in range(2):
            for args in ((0, 0, 0, 2), (0, 1, 0, 2), (1, 1, 0, 2)):
                ccopy(*args, h).wait_send()
        for q in range(2):
            for h in range(2):
                rcopy(q, h).wait_recv()
            close(back[q], q)
        for q in range(2):
            store_out(q).wait()

    @pl.when(worker)
    def _():
        lane = lax.broadcasted_iota(jnp.int32, (half_slab, LANES), 1)

        def assemble(t):
            cur[...] = wbuf[t]

            def one(c, carry):
                block = rel(c // (CI_SPLIT // F)) * (CI_SPLIT // F) + c % (CI_SPLIT // F)
                for p in range(CO_SPLIT // 2):
                    vl = cur[owner_ref[2 * p * CI_SPLIT + block]].astype(F32)
                    vr = cur[owner_ref[(2 * p + 1) * CI_SPLIT + block]].astype(F32)
                    top = jnp.where(lane < SLAB, vl, pltpu.roll(vr, SLAB, 1))
                    low = jnp.where(lane < SLAB, pltpu.roll(vl, SLAB, 1), vr)
                    pair = jnp.concatenate([top, low], axis=0).astype(BF16)
                    wt[t, pl.ds(pl.multiple_of(c * SLAB, SLAB), SLAB), p * LANES : (p + 1) * LANES] = pair
                return carry

            lax.fori_loop(0, CI_SPLIT, one, 0, unroll=4)
            wg[t, :, :rows] = wt[t, :rows]

        def build(q, img, lo, hi):
            edge = jnp.zeros((WW, LANES), F32)

            def one(k, carry):
                j = k // (rows // LANES)
                part = pl.ds(pl.multiple_of((k % (rows // LANES)) * LANES, LANES), LANES)
                dst = pl.ds(pl.multiple_of(k * LANES, LANES), LANES)
                raw = ch[img, q, j, :, part].astype(F32)
                for d in range(3):
                    if d == 1:
                        v = raw
                    else:
                        moved = pltpu.roll(raw, 1 if d == 0 else pixels - 1, 0)
                        v = jnp.where(mask[d // 2] > 0, moved, 0.0)
                    at = img * pitch
                    win[q, 1, d, pl.ds(pl.multiple_of(at, 16), pixels), dst] = v.astype(BF16)
                    tall = jnp.concatenate([edge, v, edge], axis=0).astype(BF16)
                    win[q, 0, d, pl.ds(pl.multiple_of(at, 16), pitch), dst] = tall
                return carry

            lax.fori_loop(lo, hi, one, 0)

        def conv(t, carry):
            r, c = t // 3, t % 3
            start = pl.multiple_of(r // 2 * 2 * WW, 16)
            acc_c[...] += jnp.dot(win[0, r % 2, c, pl.ds(start, both), :], wt[t], preferred_element_type=F32)
            return carry

        def grads(img, lo, n):
            at = pl.ds(pl.multiple_of(lo * rows, rows), n * rows)

            def one(t, carry):
                r, c = 2 - t // 3, 2 - t % 3
                start = pl.multiple_of(img * pitch + r // 2 * 2 * WW, 16)
                acc_g[img] += lax.dot_general(
                    win[1, r % 2, c, pl.ds(start, pixels), at], wg[t, :, at],
                    (((1,), (1,)), ((), ())), preferred_element_type=F32,
                )
                return carry

            return one

        def wex_half(t, h):
            for j in range(1, F):
                xcopy(t, j, h).wait_recv()

        def wex(t, carry):
            for h in range(2):
                wex_half(t, h)
            return carry

        def own(t):
            for h in range(2):
                fcopy(t, me, 1, across, h).start()

        def forward(t):
            for h in range(2):
                fcopy(t, mate, 0, mate, h).wait_recv()
                fcopy(t, mate, 2, across, h).start()

        own(0)
        spread(0)
        csend_all(1, 0, 0, 2)
        csend_all(1, 0, 0, 1)
        pack(1)
        spread(1)
        csend_all(1, 1, 0, 3)
        csend_all(1, 1, 0, 1)
        pack_rest(2)
        forward(0)
        own(1)
        acc_c[...] = jnp.zeros_like(acc_c)
        acc_g[...] = jnp.zeros_like(acc_g)
        for q in range(2):
            for d in range(3):
                win[q, 1, d, pixels:pitch] = jnp.zeros((pitch - pixels, F * rows), BF16)
        col = lax.broadcasted_iota(jnp.int32, (pixels, LANES), 0) % WW
        mask[0] = jnp.where(col >= 1, 1.0, 0.0)
        mask[1] = jnp.where(col < WW - 1, 1.0, 0.0)
        make_perm()
        forward(1)
        own(2)
        carrived(1, 0, 2)
        csend_all(1, 0, 2, 1)
        carrived(1, 0, 1)
        carrived(1, 1, 1)
        parts = rows // LANES * F

        def step(t, carry):
            @pl.when((t >= 1) & (t + 1 < taps))
            def _():
                forward(t + 1)

            @pl.when((t >= 1) & (t + 2 < taps))
            def _():
                own(t + 2)

            @pl.when(t == 3)
            def _():
                carrived(0, 0, 0)
                csend_all(0, 0, 0, 1)

            @pl.when(t == 4)
            def _():
                carrived(0, 0, 2)
                csend_all(0, 0, 2, 1)

            @pl.when(t == 6)
            def _():
                carrived(0, 1, 0)
                csend_all(0, 1, 0, 1)

            for h in range(2):
                fcopy(t, across, 1, across, h).wait_recv()
                fcopy(t, far, 2, across, h).wait_recv()
            assemble(t)
            for h in range(2):
                for j in (2, 3, 1):
                    xcopy(t, j, h).start()

            @pl.when(t == 0)
            def _():
                carrived(1, 0, 3)

            @pl.when(t == 4)
            def _():
                carrived(0, 0, 1)
                carrived(0, 0, 3)

            @pl.when(t == 6)
            def _():
                carrived(0, 1, 1)

            count = jnp.where((t == 0) | (t == 4), parts, jnp.where((t == 1) | (t == 6), parts // 2, 0))
            build(jnp.where((t == 1) | (t == 6), 1, 0), jnp.where(t < 2, 1, 0), 0, count)
            first = jnp.where(t == 4, 0, jnp.where(t == 5, 3, t))
            last = jnp.where(t < 4, t, jnp.where(t == 4, 3, t + 1))
            lax.fori_loop(first, last, conv, 0)

            @pl.when(t == taps - 1)
            def _():
                ret[0] = acc_c[:pixels].astype(BF16)
                for h in range(2):
                    rcopy(0, h).start()

            lo = t - 2
            hi = jnp.where(t >= 2, t - 1, lo)
            lax.fori_loop(lo, hi, wex, 0)
            lax.fori_loop(lo, hi, grads(1, 0, F // 2), 0)
            lo0 = jnp.where(t == 6, 0, t - 2)
            hi0 = jnp.where(t >= 6, t - 1, lo0)
            lax.fori_loop(lo0, hi0, grads(0, 0, F // 2), 0)
            return carry

        lax.fori_loop(0, taps, step, 0)
        carrived(0, 1, 2)
        csend_all(0, 1, 2, 1)
        close(acc_c[pitch:].astype(BF16), 0)
        carrived(0, 1, 3)
        build(1, 0, parts // 2, parts)
        lax.fori_loop(0, taps - 2, grads(0, F // 2, F // 2), 0)
        wex(taps - 2, 0)
        lax.fori_loop(taps - 2, taps - 1, grads(0, 0, F), 0)
        t = taps - 1
        r, c = 2 - t // 3, 2 - t % 3
        for h in range(2):
            at = slice(h * LANES, (h + 1) * LANES)
            wex_half(t, h)
            end = lax.dot_general(
                win[1, r % 2, c, r // 2 * 2 * WW : r // 2 * 2 * WW + pixels], wg[t, at],
                (((1,), (1,)), ((), ())), preferred_element_type=F32,
            )
            ret[1, :, at] = (acc_g[0, :, at] + end).astype(BF16)
            rcopy(1, h).start()
        carrived(1, 1, 2)
        csend_all(1, 1, 2, 1)
        lax.fori_loop(taps - 2, taps, grads(1, 0, F // 2), 0)
        build(1, 1, parts // 2, parts * 3 // 4)
        carrived(1, 1, 3)
        build(1, 1, parts * 3 // 4, parts)
        lax.fori_loop(0, taps, grads(1, F // 2, F // 2), 0)
        close(acc_g[1].astype(BF16), 1)

        def drain(t, carry):
            for h in range(2):
                fcopy(t, me, 1, across, h).wait_send()
                fcopy(t, mate, 2, across, h).wait_send()
                for j in range(1, F):
                    xcopy(t, j, h).wait_send()
            return carry

        lax.fori_loop(0, taps, drain, 0)
        for h in range(2):
            for args in (
                (1, 0, 0, 2), (1, 0, 0, 1), (1, 1, 0, 3), (1, 1, 0, 1), (1, 0, 2, 1), (0, 0, 0, 1),
                (0, 0, 2, 1), (1, 1, 2, 1), (0, 1, 0, 1), (0, 1, 2, 1),
            ):
                ccopy(*args, h).wait_send()
            rcopy(0, h).wait_send()
            rcopy(1, h).wait_send()
        for q in range(2):
            store_out(q).wait()


def hand_over_kernel(conv_ref, grad_ref, conv_out, grad_out, sem):
    copies = [
        pltpu.make_async_copy(conv_ref, conv_out, sem.at[0]),
        pltpu.make_async_copy(grad_ref, grad_out, sem.at[1]),
    ]
    for copy in copies:
        copy.start()
    for copy in copies:
        copy.wait()


def fast_body(D, F, inputs, filters, out_grad, block_owner):
    slots, taps = filters.shape[0], filters.shape[1]
    channels, images, pixels = inputs.shape
    rows = channels // CIB * SLAB
    pitch = pixels + 2 * WW
    x, g = inputs[:, 0].T, out_grad[:, 0].T
    fl = filters.transpose(1, 2, 0, 3)
    anywhere = pl.BlockSpec(memory_space=pl.ANY)
    sm = pl.BlockSpec(memory_space=pltpu.SMEM)
    dma = pltpu.SemaphoreType.DMA
    made = pl.pallas_call(
        main_kernel,
        out_shape=[jax.ShapeDtypeStruct((pixels, channels), BF16)] * 2,
        in_specs=[anywhere, anywhere, anywhere, sm],
        out_specs=[anywhere, anywhere],
        scratch_shapes=[
            pltpu.VMEM(fl.shape, BF16),
            pltpu.VMEM((2, pixels, channels), BF16),
            pltpu.VMEM((SLAB * slots, LANES), F32),
            pltpu.VMEM((pixels, rows), F32),
            pltpu.VMEM((taps, D * slots, SLAB // 2, LANES), BF16),
            pltpu.VMEM((D * slots, SLAB // 2, LANES), BF16),
            pltpu.VMEM((taps, F * rows, rows), BF16),
            pltpu.VMEM((taps, rows, F * rows), BF16),
            pltpu.VMEM((2, 2, F, pixels, rows), BF16),
            pltpu.VMEM((2, 2, 3, 2 * pitch, F * rows), BF16),
            pltpu.VMEM((2, pixels, LANES), F32),
            pltpu.VMEM((rows, rows), BF16),
            pltpu.VMEM((pitch + pixels, rows), F32),
            pltpu.VMEM((2, pixels, rows), F32),
            pltpu.VMEM((2, pixels, rows), BF16),
            pltpu.VMEM((2, pixels, rows), BF16),
            pltpu.VMEM((2, pixels, channels), BF16),
            dma((taps,)), dma((2,)), dma((2,)), dma((3, taps, 2)), dma((3, taps, 2)), dma((3, 2, 2, F, 2)), dma((2, 2, F, 2)),
            dma((taps, F, 2)), dma((taps, F, 2)), dma((2, 2)), dma((2, 2)),
        ],
        compiler_params=pltpu.CompilerParams(
            collective_id=0, has_side_effects=True, vmem_limit_bytes=62 * 1024 * 1024
        ),
    )(x, g, fl, block_owner)
    conv, grad = pl.pallas_call(
        hand_over_kernel,
        out_shape=[jax.ShapeDtypeStruct((pixels, channels), BF16)] * 2,
        in_specs=[anywhere, anywhere],
        out_specs=[anywhere, anywhere],
        scratch_shapes=[dma((2,))],
    )(*made)
    return conv.T[:, None], grad.T[:, None]


def solution(mesh):
    D, F = mesh.shape["dp"], mesh.shape["filt"]
    placed = (
        P("filt", ("parts", "dp"), None),
        P(("parts", "dp"), None, None, "filt"),
        P("filt", ("parts", "dp"), None),
        P("parts"),
    )

    def body(inputs, filters, out_grad, block_owner):
        if D == 4 and F == 4 and filters.shape[0] % 16 == 0 and inputs.shape[1] == 1:
            return fast_body(D, F, inputs, filters, out_grad, block_owner)
        return plain_body(inputs, filters, out_grad, block_owner)

    return jax.shard_map(
        body,
        mesh=mesh,
        in_specs=placed,
        out_specs=(P("filt", ("parts", "dp"), None), P("filt", ("parts", "dp"), None)),
        check_vma=False,
    )
```

```python
import functools

import jax
import jax.numpy as jnp
from jax import lax
from jax.experimental import pallas as pl
from jax.experimental.pallas import tpu as pltpu
from jax.sharding import PartitionSpec as P

GW = 1008
HH = 24
WW = 24
CO_SPLIT = 4
CI_SPLIT = 16
CIB = 63
TAPS = 9
SLAB = 64
LANES = 128
MESH = pl.DeviceIdType.MESH
F32 = jnp.float32
BF16 = jnp.bfloat16


def tap_window(flat, shift_row, shift_col):
    padded = jnp.pad(flat, ((0, 0), (0, 0), (WW + 1, WW + 1)))
    begin = WW + 1 + (shift_row - 1) * WW + (shift_col - 1)
    piece = padded[:, :, begin : begin + HH * WW]
    column = jnp.arange(HH * WW, dtype=jnp.int32) % WW + (shift_col - 1)
    valid = (column >= 0) & (column < WW)
    piece = jnp.where(valid[None, None, :], piece, jnp.zeros_like(piece))
    return piece.reshape(flat.shape[0], flat.shape[1] * HH * WW)


def plain_body(inputs, filters, out_grad, block_owner):
    slot_data = lax.all_gather(filters, "dp", axis=0, tiled=True)
    blocks = lax.map(lambda b: lax.dynamic_index_in_dim(slot_data, b, 0, False), block_owner)
    col_block = filters.shape[3]
    w_local = blocks.reshape(CO_SPLIT, CI_SPLIT, TAPS, CIB, col_block)
    w_local = w_local.transpose(2, 1, 3, 0, 4).reshape(TAPS, GW, CO_SPLIT * col_block)
    image_total = inputs.shape[1]
    pixel_span = image_total * HH * WW
    running = jnp.zeros((w_local.shape[2], pixel_span), F32)
    portion = lax.all_gather(inputs, "filt", axis=0, tiled=True)
    for offset in range(TAPS):
        window = tap_window(portion, offset // 3, offset % 3)
        running = running + lax.dot_general(
            w_local[offset], window, (((0,), (0,)), ((), ())), preferred_element_type=F32
        )
    conv_out = running.reshape(running.shape[0], image_total, HH * WW).astype(BF16)
    total_sum = jnp.zeros((inputs.shape[0] * lax.axis_size("filt"), pixel_span), F32)
    for offset in range(TAPS):
        window = tap_window(out_grad, 2 - offset // 3, 2 - offset % 3)
        total_sum = total_sum + jnp.dot(w_local[offset], window, preferred_element_type=F32)
    result = lax.psum_scatter(total_sum, "filt", scatter_dimension=0, tiled=True)
    in_grad = result.reshape(result.shape[0], image_total, HH * WW).astype(BF16)
    return (conv_out, in_grad)


def main_kernel(
    x_ref, g_ref, f_ref, owner_ref, conv_ref, grad_ref,
    fbuf, xin, tmp2, tmp, wbuf, cur, wt, wg, ch, win, mask, perm, acc_c, acc_g, ret, back, outb,
    fsem, isem, osem, wsend, zsend, wrecv, csend, crecv, xsend, xrecv, rsend, rrecv,
):
    me = lax.axis_index("dp")
    f = lax.axis_index("filt")
    taps, rows_in, slots, cols_in = f_ref.shape
    pixels, channels = x_ref.shape
    rows = acc_g.shape[2]
    pitch = pixels + 2 * WW
    F = wg.shape[5] // rows
    half_slab, strip = SLAB // 2, wbuf.shape[3]
    fx, fc = f // 2, f % 2

    def rel(j):
        j1, j2 = j % 2, j // 2
        return 2 * (fx + j2 - 2 * fx * j2) + (fc + j1 - 2 * fc * j1)

    mate = me + 1 - 2 * (me % 2)
    across = 3 - me
    im = ((me + 1) // 2) % 2
    worker = im == 1

    load_first = pltpu.make_async_copy(f_ref.at[0], fbuf.at[0], fsem.at[0])
    load_rest = pltpu.make_async_copy(f_ref.at[pl.ds(1, taps - 1)], fbuf.at[pl.ds(1, taps - 1)], fsem.at[1])

    def load_in(q):
        return pltpu.make_async_copy((x_ref, g_ref)[q], xin.at[q], isem.at[q])

    def store_out(q):
        return pltpu.make_async_copy(outb.at[q], (conv_ref, grad_ref)[q], osem.at[q])

    load_first.start()
    barrier = pltpu.get_barrier_semaphore()
    for j in range(1, F):
        pl.semaphore_signal(barrier, inc=1, device_id={"filt": rel(j)}, device_id_type=MESH)
    pl.semaphore_signal(barrier, inc=1, device_id={"dp": mate}, device_id_type=MESH)

    @pl.when(worker)
    def _():
        pl.semaphore_signal(barrier, inc=1, device_id={"dp": across}, device_id_type=MESH)

    load_rest.start()
    for q in range(2):
        load_in(q).start()

    def remote(src, dst, send, recv, device):
        return pltpu.make_async_remote_copy(
            src_ref=src, dst_ref=dst, send_sem=send, recv_sem=recv, device_id=device, device_id_type=MESH
        )

    def fcopy(t, o, kind, to, h, send):
        part = wbuf.at[t, h, pl.ds(o * slots, slots)]
        return remote(part, part, send, wrecv.at[kind, t, h], {"dp": to})

    def far_pair(t, h):
        part = wbuf.at[t, h, pl.ds(across // 2 * 2 * slots, 2 * slots)]
        return remote(part, part, wsend.at[0], wrecv.at[1, t, h], {"dp": across})

    def sent_pair():
        part = wbuf.at[:, :, pl.ds(me // 2 * 2 * slots, 2 * slots)]
        return remote(part, part, wsend.at[0], wrecv.at[1, 0, 0], {"dp": across})

    def ccopy(img, q, j, k, h, send):
        if k == 3:
            to, device = j, {"dp": mate}
        else:
            to, device = j ^ k, {"filt": rel(k)}
        part = pl.ds(h * (pixels // 2), pixels // 2)
        return remote(ch.at[img, q, j, part], ch.at[img, q, to, part], send, crecv.at[img, q, to], device)

    def csend_all(img, q, j, k):
        for h in range(2):
            ccopy(img, q, j, k, h, csend.at[1 if (img, q) == (0, 1) else 0]).start()

    def csent(part, k):
        remote(part, part, csend.at[k], crecv.at[0, 0, 0], {"filt": rel(1)}).wait_send()

    def carrived(img, q, j):
        part = ch.at[img, q, j]
        remote(part, part, csend.at[0], crecv.at[img, q, j], {"filt": rel(1)}).wait_recv()

    def xcopy(t, j, h):
        return remote(
            wt.at[t, pl.ds(j * (CI_SPLIT // F), CI_SPLIT // F), :, h], wg.at[t, h, :, :, :, pl.ds(j * rows, rows)],
            xsend.at[0], xrecv.at[t, h], {"filt": rel(j)},
        )

    others = pl.ds(rows, (F - 1) * rows)

    def rcopy(q, h):
        return remote(ret.at[q, h], back.at[q, h], rsend.at[0], rrecv.at[q, h], {"dp": mate})

    tmp2[...] = jnp.zeros_like(tmp2)

    def pack(t):
        tmp2[: rows_in * slots, :cols_in] = fbuf[t].astype(F32).reshape(rows_in * slots, cols_in)
        for s in range(slots):
            lo = tmp2[pl.ds(s, half_slab, stride=slots), :]
            hi = tmp2[pl.ds(half_slab * slots + s, half_slab, stride=slots), :]
            both_halves = (lo + pltpu.roll(hi, SLAB, 1)).astype(BF16)
            for h in range(2):
                wbuf[t, h, me * slots + s] = both_halves[h * strip : (h + 1) * strip]

    def pack_rest(lo):
        def one(t, carry):
            pack(t)
            return carry

        lax.fori_loop(lo, taps, one, 0)

    tmp[...] = jnp.zeros_like(tmp)
    chan = lax.broadcasted_iota(jnp.int32, (pixels, rows), 1)

    def spread(q):
        load_in(q).wait()
        tmp[:, :channels] = xin[q].astype(F32)
        raw = tmp[...]
        v = jnp.zeros_like(raw)
        for k in range(channels // CIB):
            moved = raw if k == 0 else pltpu.roll(raw, k, 1)
            v = jnp.where((chan >= k * SLAB) & (chan < k * SLAB + CIB), moved, v)
        ch[im, q, 0] = v.astype(BF16)

    def close(left, right, q):
        v = jnp.dot(left, perm[q, :LANES], preferred_element_type=F32)
        v = v + jnp.dot(right, perm[q, LANES:], preferred_element_type=F32)
        outb[q] = v.astype(BF16)[:, :channels]
        store_out(q).start()

    def make_perm():
        src = lax.broadcasted_iota(jnp.int32, (rows, rows), 0)
        dst = lax.broadcasted_iota(jnp.int32, (rows, rows), 1)
        h, group, part, at = src // LANES, src % LANES // half_slab, src % half_slab // strip, src % strip
        for q, lane_of in enumerate((src, group * SLAB + part * half_slab + h * strip + at)):
            hit = jnp.zeros((rows, rows), F32)
            for k in range(channels // CIB):
                hit = jnp.where((lane_of - dst == k) & (dst >= k * CIB) & (dst < (k + 1) * CIB), 1.0, hit)
            perm[q] = hit.astype(BF16)

    load_first.wait()
    pack(0)
    pl.semaphore_wait(barrier, F + im)

    @pl.when(im == 0)
    def _():
        flight = []

        def go(make):
            if len(flight) >= 3:
                flight[len(flight) - 3].wait_send()
            copy = make(zsend.at[len(flight) % 4])
            copy.start()
            flight.append(copy)

        def tap(t):
            for h in range(2):
                go(functools.partial(fcopy, t, me, 0, mate, h))

        def chunk(img, q, j, *halves):
            for h in halves:
                go(functools.partial(ccopy, img, q, j, 3, h))

        tap(0)
        spread(0)
        csend_all(0, 0, 0, 2)
        load_rest.wait()
        pack(1)
        tap(1)
        spread(1)
        csend_all(0, 1, 0, 2)
        pack_rest(2)
        tap(2)
        chunk(0, 0, 0, 0, 1)
        carrived(1, 1, 0)
        csend_all(1, 1, 0, 2)
        tap(3)
        carrived(0, 0, 2)
        chunk(0, 0, 2, 0)
        tap(4)
        chunk(0, 0, 2, 1)
        tap(5)
        chunk(0, 1, 0, 0)
        tap(6)
        chunk(0, 1, 0, 1)
        tap(7)
        tap(8)
        carrived(0, 1, 2)
        chunk(0, 1, 2, 0, 1)
        carrived(1, 1, 2)
        chunk(1, 1, 2, 0, 1)
        make_perm()
        for copy in flight[-3:]:
            copy.wait_send()
        csent(ch.at[0, 0, pl.ds(0, 2)], 0)
        csent(ch.at[0, 1, 0], 1)
        for q in range(2):
            for h in range(2):
                rcopy(q, h).wait_recv()
            close(back[q, 0], back[q, 1], q)
        for q in range(2):
            store_out(q).wait()

    @pl.when(worker)
    def _():
        lane = lax.broadcasted_iota(jnp.int32, (strip, LANES), 1)

        def assemble(t, h):
            cur[...] = wbuf[t, h]

            def one(c, carry):
                block = rel(c // (CI_SPLIT // F)) * (CI_SPLIT // F) + c % (CI_SPLIT // F)
                for p in range(CO_SPLIT // 2):
                    vl = cur[owner_ref[2 * p * CI_SPLIT + block]].astype(F32)
                    vr = cur[owner_ref[(2 * p + 1) * CI_SPLIT + block]].astype(F32)
                    at = slice(p * LANES, (p + 1) * LANES)
                    wt[t, c, 0, h, :, at] = jnp.where(lane < SLAB, vl, pltpu.roll(vr, SLAB, 1)).astype(BF16)
                    wt[t, c, 1, h, :, at] = jnp.where(lane < SLAB, pltpu.roll(vl, SLAB, 1), vr).astype(BF16)
                return carry

            lax.fori_loop(0, CI_SPLIT, one, 0, unroll=4)
            wg[t, h, :, :, :, :rows] = wt[t, : CI_SPLIT // F, :, h]

        def build(q, img, lo, hi):
            edge = jnp.zeros((WW, LANES), F32)

            def one(k, carry):
                j = k // (rows // LANES)
                part = pl.ds(pl.multiple_of((k % (rows // LANES)) * LANES, LANES), LANES)
                dst = pl.ds(pl.multiple_of(k * LANES, LANES), LANES)
                raw = ch[img, q, j, :, part].astype(F32)
                for d in range(3):
                    if d == 1:
                        v = raw
                    else:
                        moved = pltpu.roll(raw, 1 if d == 0 else pixels - 1, 0)
                        v = jnp.where(mask[d // 2] > 0, moved, 0.0)
                    at = img * pitch
                    win[q, 1, d, pl.ds(pl.multiple_of(at, 16), pixels), dst] = v.astype(BF16)
                    tall = jnp.concatenate([edge, v, edge], axis=0).astype(BF16)
                    win[q, 0, d, pl.ds(pl.multiple_of(at, 16), pitch), dst] = tall
                return carry

            lax.fori_loop(lo, hi, one, 0)

        def conv(img):
            def one(t, carry):
                r, c = t // 3, t % 3
                start = pl.multiple_of(img * pitch + r // 2 * 2 * WW, 16)
                w = wt[t].reshape(F * rows, rows)
                acc_c[img] += jnp.dot(win[0, r % 2, c, pl.ds(start, pixels), :], w, preferred_element_type=F32)
                return carry

            return one

        def grads(img, lo, n):
            at = pl.ds(pl.multiple_of(lo * rows, rows), n * rows)

            def one(t, carry):
                r, c = 2 - t // 3, 2 - t % 3
                start = pl.multiple_of(img * pitch + r // 2 * 2 * WW, 16)
                acc_g[img] += lax.dot_general(
                    win[1, r % 2, c, pl.ds(start, pixels), at], wg[t, :, :, :, :, at].reshape(rows, n * rows),
                    (((1,), (1,)), ((), ())), preferred_element_type=F32,
                )
                return carry

            return one

        def wex_half(t, h):
            part = wg.at[t, h, :, :, :, others]
            remote(part, part, xsend.at[0], xrecv.at[t, h], {"filt": rel(1)}).wait_recv()

        def wex(t, carry):
            for h in range(2):
                wex_half(t, h)
            return carry

        def own(t):
            for h in range(2):
                fcopy(t, me, 1, across, h, wsend.at[0]).start()

        def forward(t):
            for h in range(2):
                fcopy(t, mate, 0, mate, h, wsend.at[0]).wait_recv()
                fcopy(t, mate, 1, across, h, wsend.at[0]).start()

        own(0)
        load_rest.wait()
        pack(1)
        fcopy(1, me, 1, across, 0, wsend.at[0]).start()
        spread(0)
        csend_all(1, 0, 0, 2)
        csend_all(1, 0, 0, 1)
        spread(1)
        csend_all(1, 1, 0, 3)
        csend_all(1, 1, 0, 1)
        pack_rest(2)
        forward(0)
        fcopy(1, me, 1, across, 1, wsend.at[0]).start()
        acc_c[...] = jnp.zeros_like(acc_c)
        acc_g[...] = jnp.zeros_like(acc_g)
        for q in range(2):
            for d in range(3):
                win[q, 1, d, pixels:pitch] = jnp.zeros((pitch - pixels, F * rows), BF16)
        col = lax.broadcasted_iota(jnp.int32, (pixels, LANES), 0) % WW
        mask[0] = jnp.where(col >= 1, 1.0, 0.0)
        mask[1] = jnp.where(col < WW - 1, 1.0, 0.0)
        make_perm()
        forward(1)
        own(2)
        carrived(1, 0, 2)
        csend_all(1, 0, 2, 1)
        carrived(1, 0, 1)
        carrived(1, 1, 1)
        parts = rows // LANES * F

        def step(t, carry):
            @pl.when((t >= 1) & (t + 1 < taps))
            def _():
                forward(t + 1)

            @pl.when((t >= 1) & (t + 2 < taps))
            def _():
                own(t + 2)

            @pl.when(t == 3)
            def _():
                carrived(0, 0, 0)
                csend_all(0, 0, 0, 1)

            @pl.when(t == 4)
            def _():
                carrived(0, 0, 2)
                csend_all(0, 0, 2, 1)

            @pl.when(t == 6)
            def _():
                carrived(0, 1, 0)
                csend_all(0, 1, 0, 1)

            for h in range(2):
                far_pair(t, h).wait_recv()
                assemble(t, h)
                for j in (2, 3, 1):
                    xcopy(t, j, h).start()

            @pl.when(t == 0)
            def _():
                carrived(1, 0, 3)

            @pl.when(t == 4)
            def _():
                carrived(0, 0, 1)
                carrived(0, 0, 3)

            @pl.when(t == 6)
            def _():
                carrived(0, 1, 1)

            count = jnp.where((t == 0) | (t == 4), parts, jnp.where((t == 1) | (t == 6), parts // 2, 0))
            build(jnp.where((t == 1) | (t == 6), 1, 0), jnp.where(t < 2, 1, 0), 0, count)
            first = jnp.where(t == 4, 0, jnp.where(t == 5, 3, t))
            last = jnp.where(t < 4, t, jnp.where(t == 4, 3, t + 1))
            lax.fori_loop(first, last, conv(0), 0)

            @pl.when(t == taps - 1)
            def _():
                for h in range(2):
                    ret[0, h] = acc_c[0, :, h * LANES : (h + 1) * LANES].astype(BF16)
                    rcopy(0, h).start()

            lax.fori_loop(t, jnp.where(t < taps - 1, t + 1, t), conv(1), 0)
            lo = t - 2
            hi = jnp.where((t >= 2) & (t < taps - 1), t - 1, lo)
            lax.fori_loop(lo, hi, wex, 0)
            lax.fori_loop(lo, hi, grads(1, 0, F // 2), 0)
            lo0 = jnp.where(t == 6, 0, t - 2)
            hi0 = jnp.where((t == 6) | (t == 7), t - 1, lo0)
            lax.fori_loop(lo0, hi0, grads(0, 0, F // 2), 0)
            return carry

        lax.fori_loop(0, taps, step, 0)
        carrived(0, 1, 2)
        csend_all(0, 1, 2, 1)
        lax.fori_loop(taps - 1, taps, conv(1), 0)
        wex(taps - 3, 0)
        wex(taps - 2, 0)
        lax.fori_loop(taps - 3, taps - 1, grads(0, 0, F // 2), 0)
        carrived(0, 1, 3)
        build(1, 0, parts // 2, parts)
        lax.fori_loop(0, taps - 1, grads(0, F // 2, F // 2), 0)
        t = taps - 1
        r, c = 2 - t // 3, 2 - t % 3
        for h in range(2):
            at = slice(h * LANES, (h + 1) * LANES)
            wex_half(t, h)
            end = lax.dot_general(
                win[1, r % 2, c, r // 2 * 2 * WW : r // 2 * 2 * WW + pixels], wg[t, h].reshape(LANES, F * rows),
                (((1,), (1,)), ((), ())), preferred_element_type=F32,
            )
            ret[1, h] = (acc_g[0, :, at] + end).astype(BF16)
            rcopy(1, h).start()
        carrived(1, 1, 2)
        csend_all(1, 1, 2, 1)
        close(acc_c[1, :, :LANES].astype(BF16), acc_c[1, :, LANES:].astype(BF16), 0)
        lax.fori_loop(taps - 3, taps, grads(1, 0, F // 2), 0)
        build(1, 1, parts // 2, parts * 3 // 4)
        carrived(1, 1, 3)
        build(1, 1, parts * 3 // 4, parts)
        lax.fori_loop(0, taps, grads(1, F // 2, F // 2), 0)
        close(acc_g[1, :, :LANES].astype(BF16), acc_g[1, :, LANES:].astype(BF16), 1)

        sent_pair().wait_send()
        part = wg.at[:, :, :, :, :, others]
        remote(part, part, xsend.at[0], xrecv.at[0, 0], {"filt": rel(1)}).wait_send()
        csent(ch.at[:, :, pl.ds(0, 2)], 0)
        csent(ch.at[0, 1, pl.ds(0, 2)], 1)
        remote(ret, ret, rsend.at[0], rrecv.at[0, 0], {"dp": mate}).wait_send()
        for q in range(2):
            store_out(q).wait()


def hand_over_kernel(conv_ref, grad_ref, conv_out, grad_out, held, isem, osem):
    into = [pltpu.make_async_copy(src, held.at[q], isem.at[q]) for q, src in enumerate((conv_ref, grad_ref))]
    out = [pltpu.make_async_copy(held.at[q], dst, osem.at[q]) for q, dst in enumerate((conv_out, grad_out))]
    for copy in into:
        copy.start()
    for arrive, leave in zip(into, out):
        arrive.wait()
        leave.start()
    for copy in out:
        copy.wait()


def fast_body(D, F, inputs, filters, out_grad, block_owner):
    slots, taps = filters.shape[0], filters.shape[1]
    channels, images, pixels = inputs.shape
    rows = channels // CIB * SLAB
    pitch = pixels + 2 * WW
    x, g = inputs[:, 0].T, out_grad[:, 0].T
    fl = filters.transpose(1, 2, 0, 3)
    anywhere = pl.BlockSpec(memory_space=pl.ANY)
    sm = pl.BlockSpec(memory_space=pltpu.SMEM)
    dma = pltpu.SemaphoreType.DMA
    made = pl.pallas_call(
        main_kernel,
        out_shape=[jax.ShapeDtypeStruct((pixels, channels), BF16)] * 2,
        in_specs=[anywhere, anywhere, anywhere, sm],
        out_specs=[anywhere, anywhere],
        scratch_shapes=[
            pltpu.VMEM(fl.shape, BF16),
            pltpu.VMEM((2, pixels, channels), BF16),
            pltpu.VMEM((SLAB * slots, LANES), F32),
            pltpu.VMEM((pixels, rows), F32),
            pltpu.VMEM((taps, 2, D * slots, SLAB // 4, LANES), BF16),
            pltpu.VMEM((D * slots, SLAB // 4, LANES), BF16),
            pltpu.VMEM((taps, CI_SPLIT, 2, 2, SLAB // 4, rows), BF16),
            pltpu.VMEM((taps, 2, CI_SPLIT // F, 2, SLAB // 4, F * rows), BF16),
            pltpu.VMEM((2, 2, F, pixels, rows), BF16),
            pltpu.VMEM((2, 2, 3, 2 * pitch, F * rows), BF16),
            pltpu.VMEM((2, pixels, LANES), F32),
            pltpu.VMEM((2, rows, rows), BF16),
            pltpu.VMEM((2, pixels, rows), F32),
            pltpu.VMEM((2, pixels, rows), F32),
            pltpu.VMEM((2, 2, pixels, LANES), BF16),
            pltpu.VMEM((2, 2, pixels, LANES), BF16),
            pltpu.VMEM((2, pixels, channels), BF16),
            dma((2,)), dma((2,)), dma((2,)), dma((1,)), dma((4,)), dma((2, taps, 2)), dma((2,)), dma((2, 2, F)),
            dma((1,)), dma((taps, 2)), dma((1,)), dma((2, 2)),
        ],
        compiler_params=pltpu.CompilerParams(
            collective_id=0, has_side_effects=True, vmem_limit_bytes=62 * 1024 * 1024
        ),
    )(x, g, fl, block_owner)
    conv, grad = pl.pallas_call(
        hand_over_kernel,
        out_shape=[jax.ShapeDtypeStruct((pixels, channels), BF16)] * 2,
        in_specs=[anywhere, anywhere],
        out_specs=[anywhere, anywhere],
        scratch_shapes=[pltpu.VMEM((2, pixels, channels), BF16), dma((2,)), dma((2,))],
    )(*made)
    return conv.T[:, None], grad.T[:, None]


def solution(mesh):
    D, F = mesh.shape["dp"], mesh.shape["filt"]
    placed = (
        P("filt", ("parts", "dp"), None),
        P(("parts", "dp"), None, None, "filt"),
        P("filt", ("parts", "dp"), None),
        P("parts"),
    )

    def body(inputs, filters, out_grad, block_owner):
        if D == 4 and F == 4 and filters.shape[0] % 16 == 0 and inputs.shape[1] == 1:
            return fast_body(D, F, inputs, filters, out_grad, block_owner)
        return plain_body(inputs, filters, out_grad, block_owner)

    return jax.shard_map(
        body,
        mesh=mesh,
        in_specs=placed,
        out_specs=(P("filt", ("parts", "dp"), None), P("filt", ("parts", "dp"), None)),
        check_vma=False,
    )
```

```python
import functools

import jax
import jax.numpy as jnp
from jax import lax
from jax.experimental import pallas as pl
from jax.experimental.pallas import tpu as pltpu
from jax.sharding import PartitionSpec as P

GW = 1008
HH = 24
WW = 24
CO_SPLIT = 4
CI_SPLIT = 16
CIB = 63
TAPS = 9
SLAB = 64
LANES = 128
MESH = pl.DeviceIdType.MESH
F32 = jnp.float32
BF16 = jnp.bfloat16


def tap_window(flat, shift_row, shift_col):
    padded = jnp.pad(flat, ((0, 0), (0, 0), (WW + 1, WW + 1)))
    begin = WW + 1 + (shift_row - 1) * WW + (shift_col - 1)
    piece = padded[:, :, begin : begin + HH * WW]
    column = jnp.arange(HH * WW, dtype=jnp.int32) % WW + (shift_col - 1)
    valid = (column >= 0) & (column < WW)
    piece = jnp.where(valid[None, None, :], piece, jnp.zeros_like(piece))
    return piece.reshape(flat.shape[0], flat.shape[1] * HH * WW)


def plain_body(inputs, filters, out_grad, block_owner):
    slot_data = lax.all_gather(filters, "dp", axis=0, tiled=True)
    blocks = lax.map(lambda b: lax.dynamic_index_in_dim(slot_data, b, 0, False), block_owner)
    col_block = filters.shape[3]
    w_local = blocks.reshape(CO_SPLIT, CI_SPLIT, TAPS, CIB, col_block)
    w_local = w_local.transpose(2, 1, 3, 0, 4).reshape(TAPS, GW, CO_SPLIT * col_block)
    image_total = inputs.shape[1]
    pixel_span = image_total * HH * WW
    running = jnp.zeros((w_local.shape[2], pixel_span), F32)
    portion = lax.all_gather(inputs, "filt", axis=0, tiled=True)
    for offset in range(TAPS):
        window = tap_window(portion, offset // 3, offset % 3)
        running = running + lax.dot_general(
            w_local[offset], window, (((0,), (0,)), ((), ())), preferred_element_type=F32
        )
    conv_out = running.reshape(running.shape[0], image_total, HH * WW).astype(BF16)
    total_sum = jnp.zeros((inputs.shape[0] * lax.axis_size("filt"), pixel_span), F32)
    for offset in range(TAPS):
        window = tap_window(out_grad, 2 - offset // 3, 2 - offset % 3)
        total_sum = total_sum + jnp.dot(w_local[offset], window, preferred_element_type=F32)
    result = lax.psum_scatter(total_sum, "filt", scatter_dimension=0, tiled=True)
    in_grad = result.reshape(result.shape[0], image_total, HH * WW).astype(BF16)
    return (conv_out, in_grad)


def main_kernel(
    x_ref, g_ref, f_ref, owner_ref, conv_ref, grad_ref,
    fbuf, xin, tmp2, tmp, wbuf, cur, wt, wg, ch, win, mask, perm, acc_c, acc_g, ret, back,
    fsem, isem, wsend, zsend, wrecv, csend, crecv, xsend, xrecv, rsend, rrecv,
):
    me = lax.axis_index("dp")
    f = lax.axis_index("filt")
    taps, rows_in, slots, cols_in = f_ref.shape
    pixels, channels = x_ref.shape
    rows = acc_g.shape[2]
    pitch = pixels + 2 * WW
    F = wg.shape[5] // rows
    half_slab, strip = SLAB // 2, wbuf.shape[3]
    fx, fc = f // 2, f % 2

    def rel(j):
        j1, j2 = j % 2, j // 2
        return 2 * (fx + j2 - 2 * fx * j2) + (fc + j1 - 2 * fc * j1)

    mate = me + 1 - 2 * (me % 2)
    across = 3 - me
    im = ((me + 1) // 2) % 2
    worker = im == 1

    load_first = pltpu.make_async_copy(f_ref.at[0], fbuf.at[0], fsem.at[0])
    load_rest = pltpu.make_async_copy(f_ref.at[pl.ds(1, taps - 1)], fbuf.at[pl.ds(1, taps - 1)], fsem.at[1])

    def load_in(q):
        return pltpu.make_async_copy((x_ref, g_ref)[q], xin.at[q], isem.at[q])

    load_first.start()
    barrier = pltpu.get_barrier_semaphore()
    for j in range(1, F):
        pl.semaphore_signal(barrier, inc=1, device_id={"filt": rel(j)}, device_id_type=MESH)
    pl.semaphore_signal(barrier, inc=1, device_id={"dp": mate}, device_id_type=MESH)

    @pl.when(worker)
    def _():
        pl.semaphore_signal(barrier, inc=1, device_id={"dp": across}, device_id_type=MESH)

    load_rest.start()
    for q in range(2):
        load_in(q).start()

    def remote(src, dst, send, recv, device):
        return pltpu.make_async_remote_copy(
            src_ref=src, dst_ref=dst, send_sem=send, recv_sem=recv, device_id=device, device_id_type=MESH
        )

    def fcopy(t, o, kind, to, h, send):
        part = wbuf.at[t, h, pl.ds(o * slots, slots)]
        return remote(part, part, send, wrecv.at[kind, t, h], {"dp": to})

    def far_pair(t, h):
        part = wbuf.at[t, h, pl.ds(across // 2 * 2 * slots, 2 * slots)]
        return remote(part, part, wsend.at[0], wrecv.at[1, t, h], {"dp": across})

    def sent_pair():
        part = wbuf.at[:, :, pl.ds(me // 2 * 2 * slots, 2 * slots)]
        return remote(part, part, wsend.at[0], wrecv.at[1, 0, 0], {"dp": across})

    def ccopy(img, q, j, k, h, send):
        if k == 3:
            to, device = j, {"dp": mate}
        else:
            to, device = j ^ k, {"filt": rel(k)}
        part = pl.ds(h * (pixels // 2), pixels // 2)
        return remote(ch.at[img, q, j, part], ch.at[img, q, to, part], send, crecv.at[img, q, to], device)

    def csend_all(img, q, j, k):
        for h in range(2):
            ccopy(img, q, j, k, h, csend.at[1 if (img, q) == (0, 1) else 0]).start()

    def csent(part, k):
        remote(part, part, csend.at[k], crecv.at[0, 0, 0], {"filt": rel(1)}).wait_send()

    def carrived(img, q, j):
        part = ch.at[img, q, j]
        remote(part, part, csend.at[0], crecv.at[img, q, j], {"filt": rel(1)}).wait_recv()

    def xcopy(t, j, h):
        return remote(
            wt.at[t, pl.ds(j * (CI_SPLIT // F), CI_SPLIT // F), :, h], wg.at[t, h, :, :, :, pl.ds(j * rows, rows)],
            xsend.at[0], xrecv.at[t, h], {"filt": rel(j)},
        )

    others = pl.ds(rows, (F - 1) * rows)

    def rcopy(q, h):
        return remote(ret.at[q, h], back.at[q, h], rsend.at[0], rrecv.at[q, h], {"dp": mate})

    tmp2[...] = jnp.zeros_like(tmp2)

    def pack(t):
        tmp2[: rows_in * slots, :cols_in] = fbuf[t].astype(F32).reshape(rows_in * slots, cols_in)
        for s in range(slots):
            lo = tmp2[pl.ds(s, half_slab, stride=slots), :]
            hi = tmp2[pl.ds(half_slab * slots + s, half_slab, stride=slots), :]
            both_halves = (lo + pltpu.roll(hi, SLAB, 1)).astype(BF16)
            for h in range(2):
                wbuf[t, h, me * slots + s] = both_halves[h * strip : (h + 1) * strip]

    def pack_rest(lo):
        def one(t, carry):
            pack(t)
            return carry

        lax.fori_loop(lo, taps, one, 0)

    tmp[...] = jnp.zeros_like(tmp)
    chan = lax.broadcasted_iota(jnp.int32, (pixels, rows), 1)

    def spread(q):
        load_in(q).wait()
        tmp[:, :channels] = xin[q].astype(F32)
        raw = tmp[...]
        v = jnp.zeros_like(raw)
        for k in range(channels // CIB):
            moved = raw if k == 0 else pltpu.roll(raw, k, 1)
            v = jnp.where((chan >= k * SLAB) & (chan < k * SLAB + CIB), moved, v)
        ch[im, q, 0] = v.astype(BF16)

    def close(left, right, q):
        v = jnp.dot(left, perm[q, :LANES], preferred_element_type=F32)
        v = v + jnp.dot(right, perm[q, LANES:], preferred_element_type=F32)
        (conv_ref, grad_ref)[q][...] = v.astype(BF16)[:, :channels]

    def make_perm():
        src = lax.broadcasted_iota(jnp.int32, (rows, rows), 0)
        dst = lax.broadcasted_iota(jnp.int32, (rows, rows), 1)
        h, group, part, at = src // LANES, src % LANES // half_slab, src % half_slab // strip, src % strip
        for q, lane_of in enumerate((src, group * SLAB + part * half_slab + h * strip + at)):
            hit = jnp.zeros((rows, rows), F32)
            for k in range(channels // CIB):
                hit = jnp.where((lane_of - dst == k) & (dst >= k * CIB) & (dst < (k + 1) * CIB), 1.0, hit)
            perm[q] = hit.astype(BF16)

    load_first.wait()
    pack(0)
    pl.semaphore_wait(barrier, F + im)

    @pl.when(im == 0)
    def _():
        flight = []

        def go(make):
            if len(flight) >= 3:
                flight[len(flight) - 3].wait_send()
            copy = make(zsend.at[len(flight) % 4])
            copy.start()
            flight.append(copy)

        def tap(t):
            for h in range(2):
                go(functools.partial(fcopy, t, me, 0, mate, h))

        def chunk(img, q, j, *halves):
            for h in halves:
                go(functools.partial(ccopy, img, q, j, 3, h))

        tap(0)
        spread(0)
        csend_all(0, 0, 0, 2)
        load_rest.wait()
        pack(1)
        tap(1)
        spread(1)
        csend_all(0, 1, 0, 2)
        pack_rest(2)
        tap(2)
        chunk(0, 0, 0, 0, 1)
        carrived(1, 1, 0)
        csend_all(1, 1, 0, 2)
        tap(3)
        carrived(0, 0, 2)
        chunk(0, 0, 2, 0)
        tap(4)
        chunk(0, 0, 2, 1)
        tap(5)
        chunk(0, 1, 0, 0)
        tap(6)
        chunk(0, 1, 0, 1)
        tap(7)
        tap(8)
        carrived(0, 1, 2)
        chunk(0, 1, 2, 0, 1)
        carrived(1, 1, 2)
        chunk(1, 1, 2, 0, 1)
        make_perm()
        for copy in flight[-3:]:
            copy.wait_send()
        csent(ch.at[0, 0, pl.ds(0, 2)], 0)
        csent(ch.at[0, 1, 0], 1)
        for q in range(2):
            for h in range(2):
                rcopy(q, h).wait_recv()
            close(back[q, 0], back[q, 1], q)

    @pl.when(worker)
    def _():
        lane = lax.broadcasted_iota(jnp.int32, (strip, LANES), 1)

        def assemble(t, h):
            cur[...] = wbuf[t, h]

            def one(c, carry):
                block = rel(c // (CI_SPLIT // F)) * (CI_SPLIT // F) + c % (CI_SPLIT // F)
                for p in range(CO_SPLIT // 2):
                    vl = cur[owner_ref[2 * p * CI_SPLIT + block]].astype(F32)
                    vr = cur[owner_ref[(2 * p + 1) * CI_SPLIT + block]].astype(F32)
                    at = slice(p * LANES, (p + 1) * LANES)
                    wt[t, c, 0, h, :, at] = jnp.where(lane < SLAB, vl, pltpu.roll(vr, SLAB, 1)).astype(BF16)
                    wt[t, c, 1, h, :, at] = jnp.where(lane < SLAB, pltpu.roll(vl, SLAB, 1), vr).astype(BF16)
                return carry

            lax.fori_loop(0, CI_SPLIT, one, 0, unroll=4)
            wg[t, h, :, :, :, :rows] = wt[t, : CI_SPLIT // F, :, h]

        def build(q, img, lo, hi):
            edge = jnp.zeros((WW, LANES), F32)

            def one(k, carry):
                j = k // (rows // LANES)
                part = pl.ds(pl.multiple_of((k % (rows // LANES)) * LANES, LANES), LANES)
                dst = pl.ds(pl.multiple_of(k * LANES, LANES), LANES)
                raw = ch[img, q, j, :, part].astype(F32)
                for d in range(3):
                    if d == 1:
                        v = raw
                    else:
                        moved = pltpu.roll(raw, 1 if d == 0 else pixels - 1, 0)
                        v = jnp.where(mask[d // 2] > 0, moved, 0.0)
                    at = img * pitch
                    win[q, 1, d, pl.ds(pl.multiple_of(at, 16), pixels), dst] = v.astype(BF16)
                    tall = jnp.concatenate([edge, v, edge], axis=0).astype(BF16)
                    win[q, 0, d, pl.ds(pl.multiple_of(at, 16), pitch), dst] = tall
                return carry

            lax.fori_loop(lo, hi, one, 0)

        def conv(img):
            def one(t, carry):
                r, c = t // 3, t % 3
                start = pl.multiple_of(img * pitch + r // 2 * 2 * WW, 16)
                w = wt[t].reshape(F * rows, rows)
                acc_c[img] += jnp.dot(win[0, r % 2, c, pl.ds(start, pixels), :], w, preferred_element_type=F32)
                return carry

            return one

        def grads(img, lo, n):
            at = pl.ds(pl.multiple_of(lo * rows, rows), n * rows)

            def one(t, carry):
                r, c = 2 - t // 3, 2 - t % 3
                start = pl.multiple_of(img * pitch + r // 2 * 2 * WW, 16)
                acc_g[img] += lax.dot_general(
                    win[1, r % 2, c, pl.ds(start, pixels), at], wg[t, :, :, :, :, at].reshape(rows, n * rows),
                    (((1,), (1,)), ((), ())), preferred_element_type=F32,
                )
                return carry

            return one

        def wex_half(t, h):
            part = wg.at[t, h, :, :, :, others]
            remote(part, part, xsend.at[0], xrecv.at[t, h], {"filt": rel(1)}).wait_recv()

        def wex(t, carry):
            for h in range(2):
                wex_half(t, h)
            return carry

        def own(t):
            for h in range(2):
                fcopy(t, me, 1, across, h, wsend.at[0]).start()

        def forward(t):
            for h in range(2):
                fcopy(t, mate, 0, mate, h, wsend.at[0]).wait_recv()
                fcopy(t, mate, 1, across, h, wsend.at[0]).start()

        own(0)
        load_rest.wait()
        pack(1)
        fcopy(1, me, 1, across, 0, wsend.at[0]).start()
        spread(0)
        csend_all(1, 0, 0, 2)
        csend_all(1, 0, 0, 1)
        spread(1)
        csend_all(1, 1, 0, 3)
        csend_all(1, 1, 0, 1)
        pack_rest(2)
        forward(0)
        fcopy(1, me, 1, across, 1, wsend.at[0]).start()
        acc_c[...] = jnp.zeros_like(acc_c)
        acc_g[...] = jnp.zeros_like(acc_g)
        for q in range(2):
            for d in range(3):
                win[q, 1, d, pixels:pitch] = jnp.zeros((pitch - pixels, F * rows), BF16)
        col = lax.broadcasted_iota(jnp.int32, (pixels, LANES), 0) % WW
        mask[0] = jnp.where(col >= 1, 1.0, 0.0)
        mask[1] = jnp.where(col < WW - 1, 1.0, 0.0)
        make_perm()
        forward(1)
        own(2)
        carrived(1, 0, 2)
        csend_all(1, 0, 2, 1)
        carrived(1, 0, 1)
        carrived(1, 1, 1)
        parts = rows // LANES * F

        def step(t, carry):
            for h in range(2):
                far_pair(t, h).wait_recv()
                assemble(t, h)
                for j in (2, 3, 1):
                    xcopy(t, j, h).start()

            @pl.when((t >= 1) & (t + 1 < taps))
            def _():
                forward(t + 1)

            @pl.when((t >= 1) & (t + 2 < taps))
            def _():
                own(t + 2)

            @pl.when(t == 0)
            def _():
                carrived(1, 0, 3)

            @pl.when(t == 3)
            def _():
                carrived(0, 0, 0)
                csend_all(0, 0, 0, 1)

            @pl.when(t == 4)
            def _():
                carrived(0, 0, 2)
                csend_all(0, 0, 2, 1)

            @pl.when(t == 6)
            def _():
                carrived(0, 1, 0)
                csend_all(0, 1, 0, 1)

            middle = (t > 0) & (t < taps - 1)
            lax.fori_loop(jnp.where(t == 1, 0, t), jnp.where(middle, t + 1, 0), conv(1), 0)
            lo = t - 2
            hi = jnp.where((t >= 2) & (t < taps - 1), t - 1, lo)
            lax.fori_loop(lo, hi, wex, 0)
            lax.fori_loop(lo, hi, grads(1, 0, F // 2), 0)

            @pl.when(t == 4)
            def _():
                carrived(0, 0, 1)
                carrived(0, 0, 3)

            @pl.when(t == 6)
            def _():
                carrived(0, 1, 1)

            count = jnp.where((t == 0) | (t == 4), parts, jnp.where((t == 1) | (t == 6), parts // 2, 0))
            build(jnp.where((t == 1) | (t == 6), 1, 0), jnp.where(t < 2, 1, 0), 0, count)
            first = jnp.where(t == 4, 0, jnp.where(t == 5, 3, t))
            last = jnp.where(t < 4, t, jnp.where(t == 4, 3, t + 1))
            lax.fori_loop(first, last, conv(0), 0)

            @pl.when(t == taps - 1)
            def _():
                for h in range(2):
                    ret[0, h] = acc_c[0, :, h * LANES : (h + 1) * LANES].astype(BF16)
                    rcopy(0, h).start()

            lo0 = jnp.where(t == 6, 0, t - 2)
            hi0 = jnp.where((t == 6) | (t == 7), t - 1, lo0)
            lax.fori_loop(lo0, hi0, grads(0, 0, F // 2), 0)
            return carry

        lax.fori_loop(0, taps, step, 0)
        carrived(0, 1, 2)
        csend_all(0, 1, 2, 1)
        lax.fori_loop(taps - 1, taps, conv(1), 0)
        wex(taps - 3, 0)
        wex(taps - 2, 0)
        lax.fori_loop(taps - 3, taps - 1, grads(0, 0, F // 2), 0)
        carrived(0, 1, 3)
        build(1, 0, parts // 2, parts)
        lax.fori_loop(0, taps - 1, grads(0, F // 2, F // 2), 0)
        t = taps - 1
        r, c = 2 - t // 3, 2 - t % 3
        for h in range(2):
            at = slice(h * LANES, (h + 1) * LANES)
            wex_half(t, h)
            end = lax.dot_general(
                win[1, r % 2, c, r // 2 * 2 * WW : r // 2 * 2 * WW + pixels], wg[t, h].reshape(LANES, F * rows),
                (((1,), (1,)), ((), ())), preferred_element_type=F32,
            )
            ret[1, h] = (acc_g[0, :, at] + end).astype(BF16)
            rcopy(1, h).start()
        carrived(1, 1, 2)
        csend_all(1, 1, 2, 1)
        close(acc_c[1, :, :LANES].astype(BF16), acc_c[1, :, LANES:].astype(BF16), 0)
        lax.fori_loop(taps - 3, taps, grads(1, 0, F // 2), 0)
        build(1, 1, parts // 2, parts * 3 // 4)
        carrived(1, 1, 3)
        build(1, 1, parts * 3 // 4, parts)
        lax.fori_loop(0, taps, grads(1, F // 2, F // 2), 0)
        close(acc_g[1, :, :LANES].astype(BF16), acc_g[1, :, LANES:].astype(BF16), 1)

        sent_pair().wait_send()
        part = wg.at[:, :, :, :, :, others]
        remote(part, part, xsend.at[0], xrecv.at[0, 0], {"filt": rel(1)}).wait_send()
        csent(ch.at[:, :, pl.ds(0, 2)], 0)
        csent(ch.at[0, 1, pl.ds(0, 2)], 1)
        remote(ret, ret, rsend.at[0], rrecv.at[0, 0], {"dp": mate}).wait_send()


def fast_body(D, F, inputs, filters, out_grad, block_owner):
    slots, taps = filters.shape[0], filters.shape[1]
    channels, images, pixels = inputs.shape
    rows = channels // CIB * SLAB
    pitch = pixels + 2 * WW
    x, g = inputs[:, 0].T, out_grad[:, 0].T
    fl = filters.transpose(1, 2, 0, 3)
    anywhere = pl.BlockSpec(memory_space=pl.ANY)
    vm = pl.BlockSpec(memory_space=pltpu.VMEM)
    sm = pl.BlockSpec(memory_space=pltpu.SMEM)
    dma = pltpu.SemaphoreType.DMA
    conv, grad = pl.pallas_call(
        main_kernel,
        out_shape=[pltpu.VMEM((pixels, channels), BF16)] * 2,
        in_specs=[anywhere, anywhere, anywhere, sm],
        out_specs=[vm, vm],
        scratch_shapes=[
            pltpu.VMEM(fl.shape, BF16),
            pltpu.VMEM((2, pixels, channels), BF16),
            pltpu.VMEM((SLAB * slots, LANES), F32),
            pltpu.VMEM((pixels, rows), F32),
            pltpu.VMEM((taps, 2, D * slots, SLAB // 4, LANES), BF16),
            pltpu.VMEM((D * slots, SLAB // 4, LANES), BF16),
            pltpu.VMEM((taps, CI_SPLIT, 2, 2, SLAB // 4, rows), BF16),
            pltpu.VMEM((taps, 2, CI_SPLIT // F, 2, SLAB // 4, F * rows), BF16),
            pltpu.VMEM((2, 2, F, pixels, rows), BF16),
            pltpu.VMEM((2, 2, 3, 2 * pitch, F * rows), BF16),
            pltpu.VMEM((2, pixels, LANES), F32),
            pltpu.VMEM((2, rows, rows), BF16),
            pltpu.VMEM((2, pixels, rows), F32),
            pltpu.VMEM((2, pixels, rows), F32),
            pltpu.VMEM((2, 2, pixels, LANES), BF16),
            pltpu.VMEM((2, 2, pixels, LANES), BF16),
            dma((2,)), dma((2,)), dma((1,)), dma((4,)), dma((2, taps, 2)), dma((2,)), dma((2, 2, F)),
            dma((1,)), dma((taps, 2)), dma((1,)), dma((2, 2)),
        ],
        compiler_params=pltpu.CompilerParams(
            collective_id=0, has_side_effects=True, vmem_limit_bytes=62 * 1024 * 1024
        ),
    )(x, g, fl, block_owner)
    return conv.T[:, None], grad.T[:, None]


def solution(mesh):
    D, F = mesh.shape["dp"], mesh.shape["filt"]
    placed = (
        P("filt", ("parts", "dp"), None),
        P(("parts", "dp"), None, None, "filt"),
        P("filt", ("parts", "dp"), None),
        P("parts"),
    )

    def body(inputs, filters, out_grad, block_owner):
        if D == 4 and F == 4 and filters.shape[0] % 16 == 0 and inputs.shape[1] == 1:
            return fast_body(D, F, inputs, filters, out_grad, block_owner)
        return plain_body(inputs, filters, out_grad, block_owner)

    return jax.shard_map(
        body,
        mesh=mesh,
        in_specs=placed,
        out_specs=(P("filt", ("parts", "dp"), None), P("filt", ("parts", "dp"), None)),
        check_vma=False,
    )
```

```python
import functools

import jax
import jax.numpy as jnp
from jax import lax
from jax.experimental import pallas as pl
from jax.experimental.pallas import tpu as pltpu
from jax.sharding import PartitionSpec as P

GW = 1008
HH = 24
WW = 24
CO_SPLIT = 4
CI_SPLIT = 16
CIB = 63
TAPS = 9
SLAB = 64
LANES = 128
MESH = pl.DeviceIdType.MESH
F32 = jnp.float32
BF16 = jnp.bfloat16


def tap_window(flat, shift_row, shift_col):
    padded = jnp.pad(flat, ((0, 0), (0, 0), (WW + 1, WW + 1)))
    begin = WW + 1 + (shift_row - 1) * WW + (shift_col - 1)
    piece = padded[:, :, begin : begin + HH * WW]
    column = jnp.arange(HH * WW, dtype=jnp.int32) % WW + (shift_col - 1)
    valid = (column >= 0) & (column < WW)
    piece = jnp.where(valid[None, None, :], piece, jnp.zeros_like(piece))
    return piece.reshape(flat.shape[0], flat.shape[1] * HH * WW)


def plain_body(inputs, filters, out_grad, block_owner):
    slot_data = lax.all_gather(filters, "dp", axis=0, tiled=True)
    blocks = lax.map(lambda b: lax.dynamic_index_in_dim(slot_data, b, 0, False), block_owner)
    col_block = filters.shape[3]
    w_local = blocks.reshape(CO_SPLIT, CI_SPLIT, TAPS, CIB, col_block)
    w_local = w_local.transpose(2, 1, 3, 0, 4).reshape(TAPS, GW, CO_SPLIT * col_block)
    image_total = inputs.shape[1]
    pixel_span = image_total * HH * WW
    running = jnp.zeros((w_local.shape[2], pixel_span), F32)
    portion = lax.all_gather(inputs, "filt", axis=0, tiled=True)
    for offset in range(TAPS):
        window = tap_window(portion, offset // 3, offset % 3)
        running = running + lax.dot_general(
            w_local[offset], window, (((0,), (0,)), ((), ())), preferred_element_type=F32
        )
    conv_out = running.reshape(running.shape[0], image_total, HH * WW).astype(BF16)
    total_sum = jnp.zeros((inputs.shape[0] * lax.axis_size("filt"), pixel_span), F32)
    for offset in range(TAPS):
        window = tap_window(out_grad, 2 - offset // 3, 2 - offset % 3)
        total_sum = total_sum + jnp.dot(w_local[offset], window, preferred_element_type=F32)
    result = lax.psum_scatter(total_sum, "filt", scatter_dimension=0, tiled=True)
    in_grad = result.reshape(result.shape[0], image_total, HH * WW).astype(BF16)
    return (conv_out, in_grad)


def main_kernel(
    x_ref, g_ref, f_ref, owner_ref, conv_ref, grad_ref,
    fbuf, xin, tmp2, tmp, wbuf, cur, wt, wg, ch, win, mask, perm, acc_c, acc_g, ret, back,
    fsem, isem, wsend, zsend, wrecv, csend, crecv, xsend, xrecv, rsend, rrecv,
):
    me = lax.axis_index("dp")
    f = lax.axis_index("filt")
    taps, rows_in, slots, cols_in = f_ref.shape
    pixels, channels = x_ref.shape
    rows = acc_g.shape[2]
    pitch = pixels + 2 * WW
    F = wg.shape[5] // rows
    half_slab, strip = SLAB // 2, wbuf.shape[3]
    fx, fc = f // 2, f % 2

    def rel(j):
        j1, j2 = j % 2, j // 2
        return 2 * (fx + j2 - 2 * fx * j2) + (fc + j1 - 2 * fc * j1)

    mate = me + 1 - 2 * (me % 2)
    across = 3 - me
    im = ((me + 1) // 2) % 2
    worker = im == 1

    load_first = pltpu.make_async_copy(f_ref.at[0], fbuf.at[0], fsem.at[0])
    load_rest = pltpu.make_async_copy(f_ref.at[pl.ds(1, taps - 1)], fbuf.at[pl.ds(1, taps - 1)], fsem.at[1])

    def load_in(q):
        return pltpu.make_async_copy((x_ref, g_ref)[q], xin.at[q], isem.at[q])

    load_first.start()
    barrier = pltpu.get_barrier_semaphore()
    for j in range(1, F):
        pl.semaphore_signal(barrier, inc=1, device_id={"filt": rel(j)}, device_id_type=MESH)
    pl.semaphore_signal(barrier, inc=1, device_id={"dp": mate}, device_id_type=MESH)

    @pl.when(worker)
    def _():
        pl.semaphore_signal(barrier, inc=1, device_id={"dp": across}, device_id_type=MESH)

    load_rest.start()
    for q in range(2):
        load_in(q).start()

    def remote(src, dst, send, recv, device):
        return pltpu.make_async_remote_copy(
            src_ref=src, dst_ref=dst, send_sem=send, recv_sem=recv, device_id=device, device_id_type=MESH
        )

    def fcopy(t, o, kind, to, h, send):
        part = wbuf.at[t, h, pl.ds(o * slots, slots)]
        return remote(part, part, send, wrecv.at[kind, t, h], {"dp": to})

    def far_pair(t, h):
        part = wbuf.at[t, h, pl.ds(across // 2 * 2 * slots, 2 * slots)]
        return remote(part, part, wsend.at[0], wrecv.at[1, t, h], {"dp": across})

    def sent_pair():
        part = wbuf.at[:, :, pl.ds(me // 2 * 2 * slots, 2 * slots)]
        return remote(part, part, wsend.at[0], wrecv.at[1, 0, 0], {"dp": across})

    def ccopy(img, q, j, k, h, send):
        if k == 3:
            to, device = j, {"dp": mate}
        else:
            to, device = j ^ k, {"filt": rel(k)}
        part = pl.ds(h * (pixels // 2), pixels // 2)
        return remote(ch.at[img, q, j, part], ch.at[img, q, to, part], send, crecv.at[img, q, to], device)

    def csend_all(img, q, j, k):
        for h in range(2):
            ccopy(img, q, j, k, h, csend.at[1 if (img, q) == (0, 1) else 0]).start()

    def csent(part, k):
        remote(part, part, csend.at[k], crecv.at[0, 0, 0], {"filt": rel(1)}).wait_send()

    def carrived(img, q, j):
        part = ch.at[img, q, j]
        remote(part, part, csend.at[0], crecv.at[img, q, j], {"filt": rel(1)}).wait_recv()

    def xcopy(t, j, h):
        return remote(
            wt.at[t, pl.ds(j * (CI_SPLIT // F), CI_SPLIT // F), :, h], wg.at[t, h, :, :, :, pl.ds(j * rows, rows)],
            xsend.at[0], xrecv.at[t, h], {"filt": rel(j)},
        )

    others = pl.ds(rows, (F - 1) * rows)

    def rcopy(q, h):
        return remote(ret.at[q, h], back.at[q, h], rsend.at[0], rrecv.at[q, h], {"dp": mate})

    tmp2[...] = jnp.zeros_like(tmp2)

    def pack(t):
        tmp2[: rows_in * slots, :cols_in] = fbuf[t].astype(F32).reshape(rows_in * slots, cols_in)
        for s in range(slots):
            lo = tmp2[pl.ds(s, half_slab, stride=slots), :]
            hi = tmp2[pl.ds(half_slab * slots + s, half_slab, stride=slots), :]
            both_halves = (lo + pltpu.roll(hi, SLAB, 1)).astype(BF16)
            for h in range(2):
                wbuf[t, h, me * slots + s] = both_halves[h * strip : (h + 1) * strip]

    def pack_rest(lo):
        def one(t, carry):
            pack(t)
            return carry

        lax.fori_loop(lo, taps, one, 0)

    tmp[...] = jnp.zeros_like(tmp)
    chan = lax.broadcasted_iota(jnp.int32, (pixels, rows), 1)

    def spread(q):
        load_in(q).wait()
        tmp[:, :channels] = xin[q].astype(F32)
        raw = tmp[...]
        v = jnp.zeros_like(raw)
        for k in range(channels // CIB):
            moved = raw if k == 0 else pltpu.roll(raw, k, 1)
            v = jnp.where((chan >= k * SLAB) & (chan < k * SLAB + CIB), moved, v)
        ch[im, q, 0] = v.astype(BF16)

    def close(left, right, q):
        v = jnp.dot(left, perm[q, :LANES], preferred_element_type=F32)
        v = v + jnp.dot(right, perm[q, LANES:], preferred_element_type=F32)
        (conv_ref, grad_ref)[q][...] = v.astype(BF16)[:, :channels]

    def make_perm():
        src = lax.broadcasted_iota(jnp.int32, (rows, rows), 0)
        dst = lax.broadcasted_iota(jnp.int32, (rows, rows), 1)
        h, group, part, at = src // LANES, src % LANES // half_slab, src % half_slab // strip, src % strip
        for q, lane_of in enumerate((src, group * SLAB + part * half_slab + h * strip + at)):
            hit = jnp.zeros((rows, rows), F32)
            for k in range(channels // CIB):
                hit = jnp.where((lane_of - dst == k) & (dst >= k * CIB) & (dst < (k + 1) * CIB), 1.0, hit)
            perm[q] = hit.astype(BF16)

    load_first.wait()
    pack(0)
    pl.semaphore_wait(barrier, F + im)

    @pl.when(im == 0)
    def _():
        flight = []

        def go(make):
            if len(flight) >= 3:
                flight[len(flight) - 3].wait_send()
            copy = make(zsend.at[len(flight) % 4])
            copy.start()
            flight.append(copy)

        def tap(t):
            for h in range(2):
                go(functools.partial(fcopy, t, me, 0, mate, h))

        def chunk(img, q, j, *halves):
            for h in halves:
                go(functools.partial(ccopy, img, q, j, 3, h))

        tap(0)
        spread(0)
        csend_all(0, 0, 0, 2)
        load_rest.wait()
        pack(1)
        tap(1)
        spread(1)
        csend_all(0, 1, 0, 2)
        pack_rest(2)
        tap(2)
        chunk(0, 0, 0, 0, 1)
        carrived(1, 1, 0)
        csend_all(1, 1, 0, 2)
        tap(3)
        tap(4)
        carrived(0, 0, 2)
        chunk(0, 0, 2, 0)
        tap(5)
        chunk(0, 0, 2, 1)
        tap(6)
        tap(7)
        chunk(0, 1, 0, 0)
        tap(8)
        chunk(0, 1, 0, 1)
        carrived(0, 1, 2)
        chunk(0, 1, 2, 0, 1)
        carrived(1, 1, 2)
        chunk(1, 1, 2, 0, 1)
        make_perm()
        for copy in flight[-3:]:
            copy.wait_send()
        csent(ch.at[0, 0, pl.ds(0, 2)], 0)
        csent(ch.at[0, 1, 0], 1)
        for q in range(2):
            for h in range(2):
                rcopy(q, h).wait_recv()
            close(back[q, 0], back[q, 1], q)

    @pl.when(worker)
    def _():
        lane = lax.broadcasted_iota(jnp.int32, (strip, LANES), 1)

        def assemble(t, h):
            cur[...] = wbuf[t, h]

            def one(c, carry):
                block = rel(c // (CI_SPLIT // F)) * (CI_SPLIT // F) + c % (CI_SPLIT // F)
                for p in range(CO_SPLIT // 2):
                    vl = cur[owner_ref[2 * p * CI_SPLIT + block]].astype(F32)
                    vr = cur[owner_ref[(2 * p + 1) * CI_SPLIT + block]].astype(F32)
                    at = slice(p * LANES, (p + 1) * LANES)
                    wt[t, c, 0, h, :, at] = jnp.where(lane < SLAB, vl, pltpu.roll(vr, SLAB, 1)).astype(BF16)
                    wt[t, c, 1, h, :, at] = jnp.where(lane < SLAB, pltpu.roll(vl, SLAB, 1), vr).astype(BF16)
                return carry

            lax.fori_loop(0, CI_SPLIT, one, 0, unroll=4)
            wg[t, h, :, :, :, :rows] = wt[t, : CI_SPLIT // F, :, h]

        def build(q, img, lo, hi):
            edge = jnp.zeros((WW, LANES), F32)

            def one(k, carry):
                j = k // (rows // LANES)
                part = pl.ds(pl.multiple_of((k % (rows // LANES)) * LANES, LANES), LANES)
                dst = pl.ds(pl.multiple_of(k * LANES, LANES), LANES)
                raw = ch[img, q, j, :, part].astype(F32)
                for d in range(3):
                    if d == 1:
                        v = raw
                    else:
                        moved = pltpu.roll(raw, 1 if d == 0 else pixels - 1, 0)
                        v = jnp.where(mask[d // 2] > 0, moved, 0.0)
                    at = img * pitch
                    win[q, 1, d, pl.ds(pl.multiple_of(at, 16), pixels), dst] = v.astype(BF16)
                    tall = jnp.concatenate([edge, v, edge], axis=0).astype(BF16)
                    win[q, 0, d, pl.ds(pl.multiple_of(at, 16), pitch), dst] = tall
                return carry

            lax.fori_loop(lo, hi, one, 0)

        def conv(img):
            def one(t, carry):
                r, c = t // 3, t % 3
                start = pl.multiple_of(img * pitch + r // 2 * 2 * WW, 16)
                w = wt[t].reshape(F * rows, rows)
                acc_c[img] += jnp.dot(win[0, r % 2, c, pl.ds(start, pixels), :], w, preferred_element_type=F32)
                return carry

            return one

        def grads(img, lo, n):
            at = pl.ds(pl.multiple_of(lo * rows, rows), n * rows)

            def one(t, carry):
                r, c = 2 - t // 3, 2 - t % 3
                start = pl.multiple_of(img * pitch + r // 2 * 2 * WW, 16)
                acc_g[img] += lax.dot_general(
                    win[1, r % 2, c, pl.ds(start, pixels), at], wg[t, :, :, :, :, at].reshape(rows, n * rows),
                    (((1,), (1,)), ((), ())), preferred_element_type=F32,
                )
                return carry

            return one

        def wex_half(t, h):
            part = wg.at[t, h, :, :, :, others]
            remote(part, part, xsend.at[0], xrecv.at[t, h], {"filt": rel(1)}).wait_recv()

        def wex(t, carry):
            for h in range(2):
                wex_half(t, h)
            return carry

        def own(t):
            for h in range(2):
                fcopy(t, me, 1, across, h, wsend.at[0]).start()

        def forward(t):
            for h in range(2):
                fcopy(t, mate, 0, mate, h, wsend.at[0]).wait_recv()
                fcopy(t, mate, 1, across, h, wsend.at[0]).start()

        own(0)
        load_rest.wait()
        pack(1)
        fcopy(1, me, 1, across, 0, wsend.at[0]).start()
        spread(0)
        csend_all(1, 0, 0, 2)
        csend_all(1, 0, 0, 1)
        spread(1)
        csend_all(1, 1, 0, 3)
        csend_all(1, 1, 0, 1)
        pack_rest(2)
        forward(0)
        fcopy(1, me, 1, across, 1, wsend.at[0]).start()
        acc_c[...] = jnp.zeros_like(acc_c)
        acc_g[...] = jnp.zeros_like(acc_g)
        for q in range(2):
            for d in range(3):
                win[q, 1, d, pixels:pitch] = jnp.zeros((pitch - pixels, F * rows), BF16)
        col = lax.broadcasted_iota(jnp.int32, (pixels, LANES), 0) % WW
        mask[0] = jnp.where(col >= 1, 1.0, 0.0)
        mask[1] = jnp.where(col < WW - 1, 1.0, 0.0)
        make_perm()
        forward(1)
        own(2)
        carrived(1, 0, 2)
        csend_all(1, 0, 2, 1)
        carrived(1, 0, 1)
        carrived(1, 1, 1)
        parts = rows // LANES * F

        def step(t, carry):
            def half(h):
                far_pair(t, h).wait_recv()
                assemble(t, h)
                for j in (2, 3, 1):
                    xcopy(t, j, h).start()

            half(0)

            @pl.when((t >= 1) & (t + 1 < taps))
            def _():
                forward(t + 1)

            @pl.when((t >= 1) & (t + 2 < taps))
            def _():
                own(t + 2)

            half(1)

            @pl.when(t == 0)
            def _():
                carrived(1, 0, 3)

            @pl.when(t == 3)
            def _():
                carrived(0, 0, 0)
                csend_all(0, 0, 0, 1)

            @pl.when(t == 5)
            def _():
                carrived(0, 0, 2)
                csend_all(0, 0, 2, 1)

            @pl.when(t == 7)
            def _():
                carrived(0, 1, 0)
                csend_all(0, 1, 0, 1)

            middle = (t > 0) & (t < taps - 1)
            lax.fori_loop(jnp.where(t == 1, 0, t), jnp.where(middle, t + 1, 0), conv(1), 0)
            lo = t - 2
            hi = jnp.where((t >= 2) & (t < taps - 1), t - 1, lo)
            lax.fori_loop(lo, hi, wex, 0)
            lax.fori_loop(lo, hi, grads(1, 0, F // 2), 0)

            @pl.when(t == 5)
            def _():
                carrived(0, 0, 1)
                carrived(0, 0, 3)

            @pl.when(t == 7)
            def _():
                carrived(0, 1, 1)

            count = jnp.where((t == 0) | (t == 5), parts, jnp.where((t == 1) | (t == 7), parts // 2, 0))
            build(jnp.where((t == 1) | (t == 7), 1, 0), jnp.where(t < 2, 1, 0), 0, count)
            first = jnp.where(t == 5, 0, jnp.where(t == 6, 3, jnp.where(t == 7, 6, t)))
            last = jnp.where(t < 5, t, jnp.where(t == 5, 3, jnp.where(t == 6, 6, t + 1)))
            lax.fori_loop(first, last, conv(0), 0)

            @pl.when(t == taps - 1)
            def _():
                for h in range(2):
                    ret[0, h] = acc_c[0, :, h * LANES : (h + 1) * LANES].astype(BF16)
                    rcopy(0, h).start()

            lo0 = jnp.where(t == 7, 0, t)
            hi0 = jnp.where(t == 7, t - 1, t)
            lax.fori_loop(lo0, hi0, grads(0, 0, F // 2), 0)
            return carry

        lax.fori_loop(0, taps, step, 0)
        carrived(0, 1, 2)
        csend_all(0, 1, 2, 1)
        lax.fori_loop(taps - 1, taps, conv(1), 0)
        wex(taps - 3, 0)
        wex(taps - 2, 0)
        lax.fori_loop(taps - 3, taps - 1, grads(0, 0, F // 2), 0)
        carrived(0, 1, 3)
        build(1, 0, parts // 2, parts)
        lax.fori_loop(0, taps - 1, grads(0, F // 2, F // 2), 0)
        t = taps - 1
        r, c = 2 - t // 3, 2 - t % 3
        for h in range(2):
            at = slice(h * LANES, (h + 1) * LANES)
            wex_half(t, h)
            end = lax.dot_general(
                win[1, r % 2, c, r // 2 * 2 * WW : r // 2 * 2 * WW + pixels], wg[t, h].reshape(LANES, F * rows),
                (((1,), (1,)), ((), ())), preferred_element_type=F32,
            )
            ret[1, h] = (acc_g[0, :, at] + end).astype(BF16)
            rcopy(1, h).start()
        carrived(1, 1, 2)
        csend_all(1, 1, 2, 1)
        close(acc_c[1, :, :LANES].astype(BF16), acc_c[1, :, LANES:].astype(BF16), 0)
        lax.fori_loop(taps - 3, taps, grads(1, 0, F // 2), 0)
        build(1, 1, parts // 2, parts * 3 // 4)
        carrived(1, 1, 3)
        build(1, 1, parts * 3 // 4, parts)
        lax.fori_loop(0, taps, grads(1, F // 2, F // 2), 0)
        close(acc_g[1, :, :LANES].astype(BF16), acc_g[1, :, LANES:].astype(BF16), 1)

        sent_pair().wait_send()
        part = wg.at[:, :, :, :, :, others]
        remote(part, part, xsend.at[0], xrecv.at[0, 0], {"filt": rel(1)}).wait_send()
        csent(ch.at[:, :, pl.ds(0, 2)], 0)
        csent(ch.at[0, 1, pl.ds(0, 2)], 1)
        remote(ret, ret, rsend.at[0], rrecv.at[0, 0], {"dp": mate}).wait_send()


def fast_body(D, F, inputs, filters, out_grad, block_owner):
    slots, taps = filters.shape[0], filters.shape[1]
    channels, images, pixels = inputs.shape
    rows = channels // CIB * SLAB
    pitch = pixels + 2 * WW
    x, g = inputs[:, 0].T, out_grad[:, 0].T
    fl = filters.transpose(1, 2, 0, 3)
    anywhere = pl.BlockSpec(memory_space=pl.ANY)
    vm = pl.BlockSpec(memory_space=pltpu.VMEM)
    sm = pl.BlockSpec(memory_space=pltpu.SMEM)
    dma = pltpu.SemaphoreType.DMA
    conv, grad = pl.pallas_call(
        main_kernel,
        out_shape=[pltpu.VMEM((pixels, channels), BF16)] * 2,
        in_specs=[anywhere, anywhere, anywhere, sm],
        out_specs=[vm, vm],
        scratch_shapes=[
            pltpu.VMEM(fl.shape, BF16),
            pltpu.VMEM((2, pixels, channels), BF16),
            pltpu.VMEM((SLAB * slots, LANES), F32),
            pltpu.VMEM((pixels, rows), F32),
            pltpu.VMEM((taps, 2, D * slots, SLAB // 4, LANES), BF16),
            pltpu.VMEM((D * slots, SLAB // 4, LANES), BF16),
            pltpu.VMEM((taps, CI_SPLIT, 2, 2, SLAB // 4, rows), BF16),
            pltpu.VMEM((taps, 2, CI_SPLIT // F, 2, SLAB // 4, F * rows), BF16),
            pltpu.VMEM((2, 2, F, pixels, rows), BF16),
            pltpu.VMEM((2, 2, 3, 2 * pitch, F * rows), BF16),
            pltpu.VMEM((2, pixels, LANES), F32),
            pltpu.VMEM((2, rows, rows), BF16),
            pltpu.VMEM((2, pixels, rows), F32),
            pltpu.VMEM((2, pixels, rows), F32),
            pltpu.VMEM((2, 2, pixels, LANES), BF16),
            pltpu.VMEM((2, 2, pixels, LANES), BF16),
            dma((2,)), dma((2,)), dma((1,)), dma((4,)), dma((2, taps, 2)), dma((2,)), dma((2, 2, F)),
            dma((1,)), dma((taps, 2)), dma((1,)), dma((2, 2)),
        ],
        compiler_params=pltpu.CompilerParams(
            collective_id=0, has_side_effects=True, vmem_limit_bytes=62 * 1024 * 1024
        ),
    )(x, g, fl, block_owner)
    return conv.T[:, None], grad.T[:, None]


def solution(mesh):
    D, F = mesh.shape["dp"], mesh.shape["filt"]
    placed = (
        P("filt", ("parts", "dp"), None),
        P(("parts", "dp"), None, None, "filt"),
        P("filt", ("parts", "dp"), None),
        P("parts"),
    )

    def body(inputs, filters, out_grad, block_owner):
        if D == 4 and F == 4 and filters.shape[0] % 16 == 0 and inputs.shape[1] == 1:
            return fast_body(D, F, inputs, filters, out_grad, block_owner)
        return plain_body(inputs, filters, out_grad, block_owner)

    return jax.shard_map(
        body,
        mesh=mesh,
        in_specs=placed,
        out_specs=(P("filt", ("parts", "dp"), None), P("filt", ("parts", "dp"), None)),
        check_vma=False,
    )
```

```python
import functools

import jax
import jax.numpy as jnp
from jax import lax
from jax.experimental import pallas as pl
from jax.experimental.pallas import tpu as pltpu
from jax.sharding import PartitionSpec as P

GW = 1008
HH = 24
WW = 24
CO_SPLIT = 4
CI_SPLIT = 16
CIB = 63
TAPS = 9
SLAB = 64
LANES = 128
MESH = pl.DeviceIdType.MESH
F32 = jnp.float32
BF16 = jnp.bfloat16


def tap_window(flat, shift_row, shift_col):
    padded = jnp.pad(flat, ((0, 0), (0, 0), (WW + 1, WW + 1)))
    begin = WW + 1 + (shift_row - 1) * WW + (shift_col - 1)
    piece = padded[:, :, begin : begin + HH * WW]
    column = jnp.arange(HH * WW, dtype=jnp.int32) % WW + (shift_col - 1)
    valid = (column >= 0) & (column < WW)
    piece = jnp.where(valid[None, None, :], piece, jnp.zeros_like(piece))
    return piece.reshape(flat.shape[0], flat.shape[1] * HH * WW)


def plain_body(inputs, filters, out_grad, block_owner):
    slot_data = lax.all_gather(filters, "dp", axis=0, tiled=True)
    blocks = lax.map(lambda b: lax.dynamic_index_in_dim(slot_data, b, 0, False), block_owner)
    col_block = filters.shape[3]
    w_local = blocks.reshape(CO_SPLIT, CI_SPLIT, TAPS, CIB, col_block)
    w_local = w_local.transpose(2, 1, 3, 0, 4).reshape(TAPS, GW, CO_SPLIT * col_block)
    image_total = inputs.shape[1]
    pixel_span = image_total * HH * WW
    running = jnp.zeros((w_local.shape[2], pixel_span), F32)
    portion = lax.all_gather(inputs, "filt", axis=0, tiled=True)
    for offset in range(TAPS):
        window = tap_window(portion, offset // 3, offset % 3)
        running = running + lax.dot_general(
            w_local[offset], window, (((0,), (0,)), ((), ())), preferred_element_type=F32
        )
    conv_out = running.reshape(running.shape[0], image_total, HH * WW).astype(BF16)
    total_sum = jnp.zeros((inputs.shape[0] * lax.axis_size("filt"), pixel_span), F32)
    for offset in range(TAPS):
        window = tap_window(out_grad, 2 - offset // 3, 2 - offset % 3)
        total_sum = total_sum + jnp.dot(w_local[offset], window, preferred_element_type=F32)
    result = lax.psum_scatter(total_sum, "filt", scatter_dimension=0, tiled=True)
    in_grad = result.reshape(result.shape[0], image_total, HH * WW).astype(BF16)
    return (conv_out, in_grad)


def main_kernel(
    x_ref, g_ref, f_ref, owner_ref, conv_ref, grad_ref,
    fbuf, xin, tmp2, tmp, wbuf, cur, wt, wg, ch, win, mask, perm, acc_c, acc_g, ret, back,
    fsem, isem, wsend, zsend, wrecv, csend, crecv, xsend, xrecv, rsend, rrecv,
):
    me = lax.axis_index("dp")
    f = lax.axis_index("filt")
    taps, rows_in, slots, cols_in = f_ref.shape
    pixels, channels = x_ref.shape
    rows = acc_g.shape[2]
    pitch = pixels + 2 * WW
    F = wg.shape[5] // rows
    half_slab, strip = SLAB // 2, wbuf.shape[3]
    fx, fc = f // 2, f % 2

    def rel(j):
        j1, j2 = j % 2, j // 2
        return 2 * (fx + j2 - 2 * fx * j2) + (fc + j1 - 2 * fc * j1)

    mate = me + 1 - 2 * (me % 2)
    across = 3 - me
    im = ((me + 1) // 2) % 2
    worker = im == 1

    load_first = pltpu.make_async_copy(f_ref.at[0], fbuf.at[0], fsem.at[0])
    load_rest = pltpu.make_async_copy(f_ref.at[pl.ds(1, taps - 1)], fbuf.at[pl.ds(1, taps - 1)], fsem.at[1])

    def load_in(q):
        return pltpu.make_async_copy((x_ref, g_ref)[q], xin.at[q], isem.at[q])

    load_first.start()
    barrier = pltpu.get_barrier_semaphore()
    for j in range(1, F):
        pl.semaphore_signal(barrier, inc=1, device_id={"filt": rel(j)}, device_id_type=MESH)
    pl.semaphore_signal(barrier, inc=1, device_id={"dp": mate}, device_id_type=MESH)

    @pl.when(worker)
    def _():
        pl.semaphore_signal(barrier, inc=1, device_id={"dp": across}, device_id_type=MESH)

    load_rest.start()
    for q in range(2):
        load_in(q).start()

    def remote(src, dst, send, recv, device):
        return pltpu.make_async_remote_copy(
            src_ref=src, dst_ref=dst, send_sem=send, recv_sem=recv, device_id=device, device_id_type=MESH
        )

    def fcopy(t, o, kind, to, h, send):
        part = wbuf.at[t, h, pl.ds(o * slots, slots)]
        return remote(part, part, send, wrecv.at[kind, t, h], {"dp": to})

    def far_pair(t, h):
        part = wbuf.at[t, h, pl.ds(across // 2 * 2 * slots, 2 * slots)]
        return remote(part, part, wsend.at[0], wrecv.at[1, t, h], {"dp": across})

    def sent_pair():
        part = wbuf.at[:, :, pl.ds(me // 2 * 2 * slots, 2 * slots)]
        return remote(part, part, wsend.at[0], wrecv.at[1, 0, 0], {"dp": across})

    def ccopy(img, q, j, k, h, send):
        if k == 3:
            to, device = j, {"dp": mate}
        else:
            to, device = j ^ k, {"filt": rel(k)}
        part = pl.ds(h * (pixels // 2), pixels // 2)
        return remote(ch.at[img, q, j, part], ch.at[img, q, to, part], send, crecv.at[img, q, to], device)

    def csend_all(img, q, j, k):
        for h in range(2):
            ccopy(img, q, j, k, h, csend.at[1 if (img, q) == (0, 1) else 0]).start()

    def csent(part, k):
        remote(part, part, csend.at[k], crecv.at[0, 0, 0], {"filt": rel(1)}).wait_send()

    def carrived(img, q, j):
        part = ch.at[img, q, j]
        remote(part, part, csend.at[0], crecv.at[img, q, j], {"filt": rel(1)}).wait_recv()

    def xcopy(t, j, h):
        return remote(
            wt.at[t, pl.ds(j * (CI_SPLIT // F), CI_SPLIT // F), :, h], wg.at[t, h, :, :, :, pl.ds(j * rows, rows)],
            xsend.at[0], xrecv.at[t, h], {"filt": rel(j)},
        )

    others = pl.ds(rows, (F - 1) * rows)

    def rcopy(q, h):
        return remote(ret.at[q, h], back.at[q, h], rsend.at[0], rrecv.at[q, h], {"dp": mate})

    tmp2[...] = jnp.zeros_like(tmp2)

    def pack(t):
        tmp2[: rows_in * slots, :cols_in] = fbuf[t].astype(F32).reshape(rows_in * slots, cols_in)
        for s in range(slots):
            lo = tmp2[pl.ds(s, half_slab, stride=slots), :]
            hi = tmp2[pl.ds(half_slab * slots + s, half_slab, stride=slots), :]
            both_halves = (lo + pltpu.roll(hi, SLAB, 1)).astype(BF16)
            for h in range(2):
                wbuf[t, h, me * slots + s] = both_halves[h * strip : (h + 1) * strip]

    def pack_rest(lo):
        def one(t, carry):
            pack(t)
            return carry

        lax.fori_loop(lo, taps, one, 0)

    tmp[...] = jnp.zeros_like(tmp)
    chan = lax.broadcasted_iota(jnp.int32, (pixels, rows), 1)

    def spread(q):
        load_in(q).wait()
        tmp[:, :channels] = xin[q].astype(F32)
        raw = tmp[...]
        v = jnp.zeros_like(raw)
        for k in range(channels // CIB):
            moved = raw if k == 0 else pltpu.roll(raw, k, 1)
            v = jnp.where((chan >= k * SLAB) & (chan < k * SLAB + CIB), moved, v)
        ch[im, q, 0] = v.astype(BF16)

    def close(left, right, q):
        v = jnp.dot(left, perm[q, :LANES], preferred_element_type=F32)
        v = v + jnp.dot(right, perm[q, LANES:], preferred_element_type=F32)
        (conv_ref, grad_ref)[q][...] = v.astype(BF16)[:, :channels]

    def make_perm():
        src = lax.broadcasted_iota(jnp.int32, (rows, rows), 0)
        dst = lax.broadcasted_iota(jnp.int32, (rows, rows), 1)
        h, group, part, at = src // LANES, src % LANES // half_slab, src % half_slab // strip, src % strip
        for q, lane_of in enumerate((src, group * SLAB + part * half_slab + h * strip + at)):
            hit = jnp.zeros((rows, rows), F32)
            for k in range(channels // CIB):
                hit = jnp.where((lane_of - dst == k) & (dst >= k * CIB) & (dst < (k + 1) * CIB), 1.0, hit)
            perm[q] = hit.astype(BF16)

    load_first.wait()
    pack(0)
    pl.semaphore_wait(barrier, F + im)

    @pl.when(im == 0)
    def _():
        flight = []

        def go(make):
            if len(flight) >= 3:
                flight[len(flight) - 3].wait_send()
            copy = make(zsend.at[len(flight) % 4])
            copy.start()
            flight.append(copy)

        def tap(t):
            for h in range(2):
                go(functools.partial(fcopy, t, me, 0, mate, h))

        def chunk(img, q, j, *halves):
            for h in halves:
                go(functools.partial(ccopy, img, q, j, 3, h))

        tap(0)
        spread(0)
        csend_all(0, 0, 0, 2)
        load_rest.wait()
        pack(1)
        tap(1)
        spread(1)
        csend_all(0, 1, 0, 2)
        pack_rest(2)
        tap(2)
        chunk(0, 0, 0, 0, 1)
        carrived(1, 1, 0)
        csend_all(1, 1, 0, 2)
        tap(3)
        tap(4)
        carrived(0, 0, 2)
        chunk(0, 0, 2, 0)
        tap(5)
        chunk(0, 0, 2, 1)
        tap(6)
        tap(7)
        chunk(0, 1, 0, 0)
        tap(8)
        chunk(0, 1, 0, 1)
        carrived(0, 1, 2)
        chunk(0, 1, 2, 0, 1)
        carrived(1, 1, 2)
        chunk(1, 1, 2, 0, 1)
        make_perm()
        for copy in flight[-3:]:
            copy.wait_send()
        csent(ch.at[0, 0, pl.ds(0, 2)], 0)
        csent(ch.at[0, 1, 0], 1)
        for q in range(2):
            for h in range(2):
                rcopy(q, h).wait_recv()
            close(back[q, 0], back[q, 1], q)

    @pl.when(worker)
    def _():
        lane = lax.broadcasted_iota(jnp.int32, (strip, LANES), 1)

        def assemble(t, h):
            cur[...] = wbuf[t, h]

            def one(c, carry):
                block = rel(c // (CI_SPLIT // F)) * (CI_SPLIT // F) + c % (CI_SPLIT // F)
                for p in range(CO_SPLIT // 2):
                    vl = cur[owner_ref[2 * p * CI_SPLIT + block]].astype(F32)
                    vr = cur[owner_ref[(2 * p + 1) * CI_SPLIT + block]].astype(F32)
                    at = slice(p * LANES, (p + 1) * LANES)
                    wt[t, c, 0, h, :, at] = jnp.where(lane < SLAB, vl, pltpu.roll(vr, SLAB, 1)).astype(BF16)
                    wt[t, c, 1, h, :, at] = jnp.where(lane < SLAB, pltpu.roll(vl, SLAB, 1), vr).astype(BF16)
                return carry

            lax.fori_loop(0, CI_SPLIT, one, 0, unroll=4)
            wg[t, h, :, :, :, :rows] = wt[t, : CI_SPLIT // F, :, h]

        def build(q, img, lo, hi):
            edge = jnp.zeros((WW, LANES), F32)

            def one(k, carry):
                j = k // (rows // LANES)
                part = pl.ds(pl.multiple_of((k % (rows // LANES)) * LANES, LANES), LANES)
                dst = pl.ds(pl.multiple_of(k * LANES, LANES), LANES)
                raw = ch[img, q, j, :, part].astype(F32)
                for d in range(3):
                    if d == 1:
                        v = raw
                    else:
                        moved = pltpu.roll(raw, 1 if d == 0 else pixels - 1, 0)
                        v = jnp.where(mask[d // 2] > 0, moved, 0.0)
                    at = img * pitch
                    win[q, 1, d, pl.ds(pl.multiple_of(at, 16), pixels), dst] = v.astype(BF16)
                    tall = jnp.concatenate([edge, v, edge], axis=0).astype(BF16)
                    win[q, 0, d, pl.ds(pl.multiple_of(at, 16), pitch), dst] = tall
                return carry

            lax.fori_loop(lo, hi, one, 0)

        def conv(img):
            def one(t, carry):
                r, c = t // 3, t % 3
                start = pl.multiple_of(img * pitch + r // 2 * 2 * WW, 16)
                w = wt[t].reshape(F * rows, rows)
                acc_c[img] += jnp.dot(win[0, r % 2, c, pl.ds(start, pixels), :], w, preferred_element_type=F32)
                return carry

            return one

        def grads(img, lo, n):
            at = pl.ds(pl.multiple_of(lo * rows, rows), n * rows)

            def one(t, carry):
                r, c = 2 - t // 3, 2 - t % 3
                start = pl.multiple_of(img * pitch + r // 2 * 2 * WW, 16)
                acc_g[img] += lax.dot_general(
                    win[1, r % 2, c, pl.ds(start, pixels), at], wg[t, :, :, :, :, at].reshape(rows, n * rows),
                    (((1,), (1,)), ((), ())), preferred_element_type=F32,
                )
                return carry

            return one

        def wex_half(t, h):
            part = wg.at[t, h, :, :, :, others]
            remote(part, part, xsend.at[0], xrecv.at[t, h], {"filt": rel(1)}).wait_recv()

        def wex(t, carry):
            for h in range(2):
                wex_half(t, h)
            return carry

        def own(t):
            for h in range(2):
                fcopy(t, me, 1, across, h, wsend.at[0]).start()

        def forward(t):
            for h in range(2):
                fcopy(t, mate, 0, mate, h, wsend.at[0]).wait_recv()
                fcopy(t, mate, 1, across, h, wsend.at[0]).start()

        own(0)
        load_rest.wait()
        pack(1)
        fcopy(1, me, 1, across, 0, wsend.at[0]).start()
        spread(0)
        csend_all(1, 0, 0, 2)
        csend_all(1, 0, 0, 1)
        spread(1)
        csend_all(1, 1, 0, 3)
        csend_all(1, 1, 0, 1)
        pack_rest(2)
        forward(0)
        fcopy(1, me, 1, across, 1, wsend.at[0]).start()
        acc_c[...] = jnp.zeros_like(acc_c)
        acc_g[...] = jnp.zeros_like(acc_g)
        for q in range(2):
            for d in range(3):
                win[q, 1, d, pixels:pitch] = jnp.zeros((pitch - pixels, F * rows), BF16)
        col = lax.broadcasted_iota(jnp.int32, (pixels, LANES), 0) % WW
        mask[0] = jnp.where(col >= 1, 1.0, 0.0)
        mask[1] = jnp.where(col < WW - 1, 1.0, 0.0)
        make_perm()
        forward(1)
        own(2)
        carrived(1, 0, 2)
        csend_all(1, 0, 2, 1)
        carrived(1, 0, 1)
        carrived(1, 1, 1)
        parts = rows // LANES * F

        def step(t, carry):
            def half(h):
                far_pair(t, h).wait_recv()
                assemble(t, h)
                for j in (2, 3, 1):
                    xcopy(t, j, h).start()

            half(0)

            @pl.when((t >= 1) & (t + 1 < taps))
            def _():
                forward(t + 1)

            half(1)

            @pl.when((t >= 1) & (t + 2 < taps))
            def _():
                own(t + 2)


            @pl.when(t == 0)
            def _():
                carrived(1, 0, 3)

            @pl.when(t == 3)
            def _():
                carrived(0, 0, 0)
                csend_all(0, 0, 0, 1)

            @pl.when(t == 5)
            def _():
                carrived(0, 0, 2)
                csend_all(0, 0, 2, 1)

            @pl.when(t == 7)
            def _():
                carrived(0, 1, 0)
                csend_all(0, 1, 0, 1)

            middle = (t > 0) & (t < taps - 1)
            lax.fori_loop(jnp.where(t == 1, 0, t), jnp.where(middle, t + 1, 0), conv(1), 0)
            lo = t - 2
            hi = jnp.where((t >= 2) & (t < taps - 1), t - 1, lo)
            lax.fori_loop(lo, hi, wex, 0)
            lax.fori_loop(lo, hi, grads(1, 0, F // 2), 0)

            @pl.when(t == 5)
            def _():
                carrived(0, 0, 1)
                carrived(0, 0, 3)

            @pl.when(t == 7)
            def _():
                carrived(0, 1, 1)

            count = jnp.where((t == 0) | (t == 5), parts, jnp.where((t == 1) | (t == 7), parts // 2, 0))
            build(jnp.where((t == 1) | (t == 7), 1, 0), jnp.where(t < 2, 1, 0), 0, count)
            first = jnp.where(t == 5, 0, jnp.where(t == 6, 3, jnp.where(t == 7, 6, t)))
            last = jnp.where(t < 5, t, jnp.where(t == 5, 3, jnp.where(t == 6, 6, t + 1)))
            lax.fori_loop(first, last, conv(0), 0)

            @pl.when(t == taps - 1)
            def _():
                for h in range(2):
                    ret[0, h] = acc_c[0, :, h * LANES : (h + 1) * LANES].astype(BF16)
                    rcopy(0, h).start()

            lo0 = jnp.where(t == 7, 0, t)
            hi0 = jnp.where(t == 7, t - 1, t)
            lax.fori_loop(lo0, hi0, grads(0, 0, F // 2), 0)
            return carry

        lax.fori_loop(0, taps, step, 0)
        carrived(0, 1, 2)
        csend_all(0, 1, 2, 1)
        wex(taps - 3, 0)
        wex(taps - 2, 0)
        lax.fori_loop(taps - 3, taps - 1, grads(0, 0, F // 2), 0)
        carrived(0, 1, 3)
        build(1, 0, parts // 2, parts)
        lax.fori_loop(0, taps - 1, grads(0, F // 2, F // 2), 0)
        t = taps - 1
        r, c = 2 - t // 3, 2 - t % 3
        for h in range(2):
            at = slice(h * LANES, (h + 1) * LANES)
            wex_half(t, h)
            end = lax.dot_general(
                win[1, r % 2, c, r // 2 * 2 * WW : r // 2 * 2 * WW + pixels], wg[t, h].reshape(LANES, F * rows),
                (((1,), (1,)), ((), ())), preferred_element_type=F32,
            )
            ret[1, h] = (acc_g[0, :, at] + end).astype(BF16)
            rcopy(1, h).start()
        carrived(1, 1, 2)
        csend_all(1, 1, 2, 1)
        lax.fori_loop(taps - 1, taps, conv(1), 0)
        close(acc_c[1, :, :LANES].astype(BF16), acc_c[1, :, LANES:].astype(BF16), 0)
        lax.fori_loop(taps - 3, taps, grads(1, 0, F // 2), 0)
        build(1, 1, parts // 2, parts * 3 // 4)
        carrived(1, 1, 3)
        build(1, 1, parts * 3 // 4, parts)
        lax.fori_loop(0, taps, grads(1, F // 2, F // 2), 0)
        close(acc_g[1, :, :LANES].astype(BF16), acc_g[1, :, LANES:].astype(BF16), 1)

        sent_pair().wait_send()
        part = wg.at[:, :, :, :, :, others]
        remote(part, part, xsend.at[0], xrecv.at[0, 0], {"filt": rel(1)}).wait_send()
        csent(ch.at[:, :, pl.ds(0, 2)], 0)
        csent(ch.at[0, 1, pl.ds(0, 2)], 1)
        remote(ret, ret, rsend.at[0], rrecv.at[0, 0], {"dp": mate}).wait_send()


def fast_body(D, F, inputs, filters, out_grad, block_owner):
    slots, taps = filters.shape[0], filters.shape[1]
    channels, images, pixels = inputs.shape
    rows = channels // CIB * SLAB
    pitch = pixels + 2 * WW
    x, g = inputs[:, 0].T, out_grad[:, 0].T
    fl = filters.transpose(1, 2, 0, 3)
    anywhere = pl.BlockSpec(memory_space=pl.ANY)
    vm = pl.BlockSpec(memory_space=pltpu.VMEM)
    sm = pl.BlockSpec(memory_space=pltpu.SMEM)
    dma = pltpu.SemaphoreType.DMA
    conv, grad = pl.pallas_call(
        main_kernel,
        out_shape=[pltpu.VMEM((pixels, channels), BF16)] * 2,
        in_specs=[anywhere, anywhere, anywhere, sm],
        out_specs=[vm, vm],
        scratch_shapes=[
            pltpu.VMEM(fl.shape, BF16),
            pltpu.VMEM((2, pixels, channels), BF16),
            pltpu.VMEM((SLAB * slots, LANES), F32),
            pltpu.VMEM((pixels, rows), F32),
            pltpu.VMEM((taps, 2, D * slots, SLAB // 4, LANES), BF16),
            pltpu.VMEM((D * slots, SLAB // 4, LANES), BF16),
            pltpu.VMEM((taps, CI_SPLIT, 2, 2, SLAB // 4, rows), BF16),
            pltpu.VMEM((taps, 2, CI_SPLIT // F, 2, SLAB // 4, F * rows), BF16),
            pltpu.VMEM((2, 2, F, pixels, rows), BF16),
            pltpu.VMEM((2, 2, 3, 2 * pitch, F * rows), BF16),
            pltpu.VMEM((2, pixels, LANES), F32),
            pltpu.VMEM((2, rows, rows), BF16),
            pltpu.VMEM((2, pixels, rows), F32),
            pltpu.VMEM((2, pixels, rows), F32),
            pltpu.VMEM((2, 2, pixels, LANES), BF16),
            pltpu.VMEM((2, 2, pixels, LANES), BF16),
            dma((2,)), dma((2,)), dma((1,)), dma((4,)), dma((2, taps, 2)), dma((2,)), dma((2, 2, F)),
            dma((1,)), dma((taps, 2)), dma((1,)), dma((2, 2)),
        ],
        compiler_params=pltpu.CompilerParams(
            collective_id=0, has_side_effects=True, vmem_limit_bytes=62 * 1024 * 1024
        ),
    )(x, g, fl, block_owner)
    return conv.T[:, None], grad.T[:, None]


def solution(mesh):
    D, F = mesh.shape["dp"], mesh.shape["filt"]
    placed = (
        P("filt", ("parts", "dp"), None),
        P(("parts", "dp"), None, None, "filt"),
        P("filt", ("parts", "dp"), None),
        P("parts"),
    )

    def body(inputs, filters, out_grad, block_owner):
        if D == 4 and F == 4 and filters.shape[0] % 16 == 0 and inputs.shape[1] == 1:
            return fast_body(D, F, inputs, filters, out_grad, block_owner)
        return plain_body(inputs, filters, out_grad, block_owner)

    return jax.shard_map(
        body,
        mesh=mesh,
        in_specs=placed,
        out_specs=(P("filt", ("parts", "dp"), None), P("filt", ("parts", "dp"), None)),
        check_vma=False,
    )
```
